32 devices in a mesh: grp: 2 (over y), gy: 4 (over z), gz: 2 (over x), vert: 2 (over core).
Axes of the slice: x: 2, y: 2, z: 4, core: 2. Of those that a mesh axis runs over, the one named last changes fastest.
Arguments:
- field: float32 [16, 64, 64, 512], P(('grp', 'vert'), 'gy', 'gz'), parts along dimension 0, as said below
- omega_x: float32 [512, 128], replicated, may hold values from -6 to 6
- omega_y: float32 [64, 32], replicated, may hold values from -6 to 6
- rank_x: int32 [2], P('grp'), parts along dimension 0, may hold values from 64 to 128
- rank_y: int32 [2], P('grp'), parts along dimension 0, may hold values from 16 to 32
Outputs:
- core: float32 [16, 32, 64, 128], P(('grp', 'vert'), 'gy', 'gz'), parts along dimension 0
- factor_x: float32 [1024, 128], P('grp'), parts along dimension 0
- factor_y: float32 [128, 32], P('grp'), parts along dimension 0
The draws below stay inside these ranges and needn't reach their ends.
There are 2 independent parts, one for each index of `grp`. The reference program is written for one: setup_inputs(seed, part) draws one part's arguments, and reference() takes and returns one part's arrays. A program takes and returns all parts, laid end to end along the dimension named above; an argument that names none is the same for every part. Nothing has to cross between parts.
Inputs may be any that keep to these rules, and one draw needn't show every extreme that they name: field values are finite and of order one; their spread differs between cells of the first dimension.
All inputs are finite; a program needn't handle non-finite values.
Results may differ from the reference program's by a relative error of at most 0.000086.
Values sent between devices are 32-bit elements; how exact they have to be, the bound alone decides.
No kernel may reach another device: no remote copies, remote signals or barrier semaphores. Data moves between devices by JAX's collectives and lax.ppermute only.
A program may use at most 64 MiB of HBM per device.

```python
import jax
import jax.numpy as jnp
from jax import lax

X = 512
V = 8
RX = 128
RY = 32
Y = 64
Z = 64


def draw_field(key, part):
    key_base, key_cols, key_rows, key_planes = jax.random.split(jax.random.fold_in(key, 7), 4)
    base = jax.random.normal(key_base, (V, Y, Z, X), jnp.float32)
    column_scale = jnp.exp(jax.random.uniform(key_cols, (X,), jnp.float32, 0.0, 1.39))
    row_scale = jnp.exp(jax.random.uniform(key_rows, (Y,), jnp.float32, -0.6, 0.6))
    plane_scale = jnp.exp(jax.random.uniform(key_planes, (V,), jnp.float32, -0.5, 0.5))
    return base * column_scale[None, None, None, :] * row_scale[None, :, None, None] * plane_scale[:, None, None, None]


def centred(key, dims, width, most, held_as=jnp.bfloat16):
    entries = width * jax.random.normal(key, dims, jnp.float32)
    return jnp.clip(entries, min=-most, max=most).astype(held_as)


def setup_inputs(seed: int = 0, part: int = 0) -> dict:
    seeds = jax.random.split(jax.random.key(seed), 6)
    part_splits = jax.random.split(jax.random.fold_in(seeds[5], part), 6)
    field = draw_field(jax.random.fold_in(jax.random.fold_in(seeds[5], part), 71), part)
    omega_x = centred(seeds[1], (X, RX), 1.0, 6.0, jnp.float32)
    omega_y = centred(seeds[2], (Y, RY), 1.0, 6.0, jnp.float32)
    rank_x = jax.random.randint(part_splits[3], (1,), RX // 2, RX + 1).astype(jnp.int32)
    rank_y = jax.random.randint(part_splits[4], (1,), RY // 2, RY + 1).astype(jnp.int32)
    return dict(field=field, omega_x=omega_x, omega_y=omega_y, rank_x=rank_x, rank_y=rank_y)


def orthonormal(sketch, trunc_rank):
    precise = lax.Precision.HIGHEST
    small_gram = jnp.dot(sketch.T, sketch, precision=precise)
    lower_factor = jnp.linalg.cholesky(small_gram)
    basis = lax.linalg.triangular_solve(lower_factor, sketch, left_side=False, lower=True, transpose_a=True)
    column_ids = jnp.arange(sketch.shape[1], dtype=jnp.int32)
    kept = (column_ids < trunc_rank[0]).astype(jnp.float32)
    return basis * kept[None, :]

def reference(field, omega_x, omega_y, rank_x, rank_y):
    precise = lax.Precision.HIGHEST
    flat = field.reshape(-1, X)
    gram_x = jnp.dot(flat.T, flat, precision=precise) / float(V * Y * Z)
    sketch_x = jnp.dot(gram_x, omega_x, precision=precise)
    factor_x = orthonormal(sketch_x, rank_x)
    core_x = jnp.dot(flat, factor_x, precision=precise).reshape(V, Y, Z, RX)
    gram_y = jnp.einsum('vazr,vbzr->ab', core_x, core_x, precision=precise) / float(V * Z * RX)
    sketch_y = jnp.dot(gram_y, omega_y, precision=precise)
    factor_y = orthonormal(sketch_y, rank_y)
    core = jnp.einsum('vyzr,yk->vkzr', core_x, factor_y, precision=precise)
    return (core, factor_x, factor_y)
```

```python
import jax
import jax.numpy as jnp
from jax import lax
from jax.sharding import PartitionSpec as P

HIGH = lax.Precision.HIGH
HIGHEST = lax.Precision.HIGHEST


def swap(value, axes, step):
    count = lax.axis_size(axes)
    assert count & (count - 1) == 0
    return lax.ppermute(value, axes, [(i, i ^ step) for i in range(count)])


def steps(count):
    return sorted(range(1, count), key=lambda s: -(s & 2) * 4 - s)


def by_step(blocks, me, count):
    if count == 4:
        pairs = blocks.reshape((2, 2) + blocks.shape[1:])
        pairs = jnp.where(me & 2 != 0, pairs[::-1], pairs)
        pairs = jnp.where(me & 1 != 0, pairs[:, ::-1], pairs)
        return pairs.reshape(blocks.shape)
    return jnp.take(blocks, me ^ jnp.arange(count), axis=0)


def sum_over_gy(part):
    count = lax.axis_size("gy")
    got = [swap(part, "gy", s) for s in steps(count)]
    for other in got:
        part = part + other
    return part


def sum_sketch(part):
    axes = ("gz", "vert")
    count = lax.axis_size(axes)
    me = lax.axis_index("gz") * lax.axis_size("vert") + lax.axis_index("vert")
    share = part.shape[0] // count
    cut = lambda who: lax.dynamic_slice_in_dim(part, who * share, share, 0)
    got = [swap(cut(me ^ s), axes, s) for s in steps(count)]
    mine = cut(me)
    for other in got:
        mine = mine + other
    mine = sum_over_gy(mine)
    whole = jnp.zeros_like(part)
    whole = lax.dynamic_update_slice_in_dim(whole, mine, me * share, 0)
    got = [(s, swap(mine, axes, s)) for s in steps(count)]
    for s, other in got:
        whole = lax.dynamic_update_slice_in_dim(whole, other, (me ^ s) * share, 0)
    return whole


def inverse_factor(small_gram, rank):
    lower = jnp.linalg.cholesky(small_gram)
    eye = jnp.eye(lower.shape[0], dtype=jnp.float32)
    inverse = lax.linalg.triangular_solve(lower, eye, left_side=False, lower=True, transpose_a=True)
    kept = (jnp.arange(lower.shape[0], dtype=jnp.int32) < rank[0]).astype(jnp.float32)
    return inverse * kept[None, :]


def body(field, omega_x, omega_y, rank_x, rank_y):
    planes, rows_y, rows_z, cells_x = field.shape
    ranks_x = omega_x.shape[1]
    ranks_y = omega_y.shape[1]
    n_gy = lax.axis_size("gy")
    gy = lax.axis_index("gy")
    all_planes = planes * lax.axis_size("vert")
    all_rows_y = rows_y * n_gy
    all_rows_z = rows_z * lax.axis_size("gz")
    flat = field.reshape(-1, cells_x)

    projected = jnp.dot(flat, omega_x, precision=HIGH)
    part = lax.dot_general(projected, flat, (((0,), (0,)), ((), ())), precision=HIGH)
    sketch_t = sum_sketch(part) / float(all_planes * all_rows_y * all_rows_z)

    share_z = rows_z // n_gy
    raw = lax.dot_general(flat, sketch_t, (((1,), (1,)), ((), ())), precision=HIGH)
    raw = raw.reshape(planes * rows_y, rows_z, ranks_x)
    cut = lambda who: lax.dynamic_slice_in_dim(raw, who * share_z, share_z, 1)
    chunks = [None] * n_gy
    for s in steps(n_gy):
        chunks[s] = swap(cut(gy ^ s), "gy", s)
    chunks[0] = cut(gy)

    small_gram = lax.dot_general(sketch_t, sketch_t, (((1,), (1,)), ((), ())), precision=HIGHEST)
    inverse_x = inverse_factor(small_gram, rank_x)
    factor_x = lax.dot_general(sketch_t, inverse_x, (((0,), (0,)), ((), ())), precision=HIGH)

    spread = jnp.stack(chunks).reshape(-1, ranks_x)
    spread = jnp.dot(spread, inverse_x, precision=HIGH)
    spread = spread.reshape(n_gy, planes, rows_y, share_z, ranks_x)
    local_gram_y = jnp.einsum("gvazr,hvbzr->gahb", spread, spread, precision=HIGH)
    local_gram_y = local_gram_y.reshape(all_rows_y, all_rows_y)
    omega_p = by_step(omega_y.reshape(n_gy, rows_y, ranks_y), gy, n_gy).reshape(all_rows_y, ranks_y)
    part_y = jnp.dot(local_gram_y, omega_p, precision=HIGHEST)
    part_y = by_step(part_y.reshape(n_gy, rows_y, ranks_y), gy, n_gy).reshape(all_rows_y, ranks_y)
    for axis in ("vert", "gz"):
        count = lax.axis_size(axis)
        got = [swap(part_y, axis, s) for s in steps(count)]
        for other in got:
            part_y = part_y + other
    sketch_y = sum_over_gy(part_y) / float(all_planes * all_rows_z * ranks_x)

    small_gram_y = lax.dot_general(sketch_y, sketch_y, (((0,), (0,)), ((), ())), precision=HIGHEST)
    inverse_y = inverse_factor(small_gram_y, rank_y)
    factor_y = jnp.dot(sketch_y, inverse_y, precision=HIGHEST)

    share_k = ranks_y // n_gy
    weights = by_step(factor_y.reshape(n_gy, rows_y, ranks_y), gy, n_gy)
    weights = weights.reshape(n_gy, rows_y, n_gy, share_k)
    weights = jnp.moveaxis(by_step(jnp.moveaxis(weights, 2, 0), gy, n_gy), 0, 2)
    mixed = jnp.einsum("gvyzr,gyhk->hvkzr", spread, weights, precision=HIGH)
    pieces = [None] * n_gy
    for s in steps(n_gy):
        pieces[s] = swap(mixed[s], "gy", s)
    pieces[0] = mixed[0]
    core = by_step(jnp.stack(pieces), gy, n_gy)
    core = jnp.moveaxis(core, 0, 2).reshape(planes, share_k, rows_z, ranks_x)
    return (core, factor_x, factor_y)


def solution(mesh):
    in_specs = (P(("grp", "vert"), "gy", "gz", None), P(), P(), P("grp"), P("grp"))
    out_specs = (P(("grp", "vert"), "gy", "gz", None), P("grp", None), P("grp", None))
    return jax.shard_map(body, mesh=mesh, in_specs=in_specs, out_specs=out_specs, check_vma=False)
```

```python
import functools

import jax
import jax.numpy as jnp
from jax import lax
from jax.experimental import pallas as pl
from jax.experimental.pallas import tpu as pltpu
from jax.sharding import PartitionSpec as P

HIGH = lax.Precision.HIGH
HIGHEST = lax.Precision.HIGHEST


def swap(value, axes, step):
    count = lax.axis_size(axes)
    assert count & (count - 1) == 0
    return lax.ppermute(value, axes, [(i, i ^ step) for i in range(count)])


def steps(count):
    return sorted(range(1, count), key=lambda s: -(s & 2) * 4 - s)


def by_step(blocks, me, count):
    if count == 4:
        pairs = blocks.reshape((2, 2) + blocks.shape[1:])
        pairs = jnp.where(me & 2 != 0, pairs[::-1], pairs)
        pairs = jnp.where(me & 1 != 0, pairs[:, ::-1], pairs)
        return pairs.reshape(blocks.shape)
    return jnp.take(blocks, me ^ jnp.arange(count), axis=0)


def sum_over_gy(part):
    count = lax.axis_size("gy")
    got = [swap(part, "gy", s) for s in steps(count)]
    for other in got:
        part = part + other
    return part


def sum_sketch(part):
    axes = ("gz", "vert")
    count = lax.axis_size(axes)
    me = lax.axis_index("gz") * lax.axis_size("vert") + lax.axis_index("vert")
    share = part.shape[0] // count
    cut = lambda who: lax.dynamic_slice_in_dim(part, who * share, share, 0)
    got = [swap(cut(me ^ s), axes, s) for s in steps(count)]
    mine = cut(me)
    for other in got:
        mine = mine + other
    mine = sum_over_gy(mine)
    whole = jnp.zeros_like(part)
    whole = lax.dynamic_update_slice_in_dim(whole, mine, me * share, 0)
    got = [(s, swap(mine, axes, s)) for s in steps(count)]
    for s, other in got:
        whole = lax.dynamic_update_slice_in_dim(whole, other, (me ^ s) * share, 0)
    return whole


def dims(left, right):
    return (((left,), (right,)), ((), ()))


def mxu(a, b, numbers):
    return lax.dot_general(a, b, numbers, preferred_element_type=jnp.float32)


def exact(a, b, numbers):
    return lax.dot_general(a, b, numbers, precision=HIGHEST, preferred_element_type=jnp.float32)


def halves(value):
    high = value.astype(jnp.bfloat16)
    return high, (value - high.astype(jnp.float32)).astype(jnp.bfloat16)


def vmem(count):
    return [pl.BlockSpec(memory_space=pltpu.VMEM)] * count


def sketch_kernel(field_ref, omega_ref, out_ref, wide, narrow):
    width = omega_ref.shape[1]
    high, low = halves(field_ref[...])
    omega_high, omega_low = halves(omega_ref[...])
    both = mxu(high, jnp.concatenate([omega_high, omega_low], axis=1), dims(1, 0))
    projected = both[:, :width] + (both[:, width:] + mxu(low, omega_high, dims(1, 0)))
    proj_high, proj_low = halves(projected)
    first = mxu(jnp.concatenate([proj_high, proj_low], axis=1), high, dims(0, 0))
    second = mxu(proj_high, low, dims(0, 0))

    @pl.when(pl.program_id(0) == 0)
    def _():
        wide[...] = first
        narrow[...] = second

    @pl.when(pl.program_id(0) > 0)
    def _():
        wide[...] += first
        narrow[...] += second

    @pl.when(pl.program_id(0) == pl.num_programs(0) - 1)
    def _():
        out_ref[...] = wide[:width, :] + (wide[width:, :] + narrow[...])


def sketch_part(flat, omega):
    rows, cells = flat.shape
    width = omega.shape[1]
    block = 512
    return pl.pallas_call(
        sketch_kernel,
        grid=(rows // block,),
        in_specs=[
            pl.BlockSpec((block, cells), lambda i: (i, 0)),
            pl.BlockSpec((cells, width), lambda i: (0, 0)),
        ],
        out_specs=pl.BlockSpec((width, cells), lambda i: (0, 0)),
        out_shape=jax.ShapeDtypeStruct((width, cells), jnp.float32),
        scratch_shapes=[pltpu.VMEM((2 * width, cells), jnp.float32), pltpu.VMEM((width, cells), jnp.float32)],
        name="sketch",
    )(flat, omega)


def chunk_kernel(where_ref, field_ref, sketch_ref, out_ref):
    width = sketch_ref.shape[0]
    rows, share, cells = field_ref.shape
    high, low = halves(field_ref[...].reshape(rows * share, cells))
    sketch_high, sketch_low = halves(sketch_ref[...])
    both = mxu(high, jnp.concatenate([sketch_high, sketch_low], axis=0), dims(1, 1))
    raw = both[:, :width] + (both[:, width:] + mxu(low, sketch_high, dims(1, 1)))
    out_ref[...] = raw.reshape(rows, share, width)


def field_chunk(where, field, sketch_t, share):
    rows, _, cells = field.shape
    width = sketch_t.shape[0]
    block = rows // 2
    return pl.pallas_call(
        chunk_kernel,
        grid_spec=pltpu.PrefetchScalarGridSpec(
            num_scalar_prefetch=1,
            grid=(rows // block,),
            in_specs=[
                pl.BlockSpec((block, share, cells), lambda i, w: (i, w[0], 0)),
                pl.BlockSpec((width, cells), lambda i, w: (0, 0)),
            ],
            out_specs=pl.BlockSpec((block, share, width), lambda i, w: (i, 0, 0)),
        ),
        out_shape=jax.ShapeDtypeStruct((rows, share, width), jnp.float32),
        name="chunk",
    )(where, field, sketch_t)


def eliminate(gram, count, rank, out_ref):
    lanes = lax.broadcasted_iota(jnp.int32, (8, count), 1)
    subs = lax.broadcasted_iota(jnp.int32, (8, count), 0)
    blocks = count // 8
    full = lambda x: jnp.broadcast_to(x, (8, count))
    left = [gram[8 * b:8 * b + 8, :] for b in range(blocks)]
    right = [(lanes == subs + 8 * b).astype(jnp.float32) for b in range(blocks)]
    for j in range(0, count, 2):
        b, s = divmod(j, 8)
        l0, l1 = full(left[b][s:s + 1, :]), full(left[b][s + 1:s + 2, :])
        r0, r1 = full(right[b][s:s + 1, :]), full(right[b][s + 1:s + 2, :])
        p, q, t = full(l0[:, j:j + 1]), full(l0[:, j + 1:j + 2]), full(l1[:, j + 1:j + 2])
        inv = 1.0 / (p * t - q * q)
        ratio = q / p
        first = r0 * lax.rsqrt(p)
        second = (r1 - ratio * r0) * lax.rsqrt(t - q * ratio)
        out_ref[j:j + 1, :] = jnp.where(j < rank, first[0:1], 0.0)
        out_ref[j + 1:j + 2, :] = jnp.where(j + 1 < rank, second[0:1], 0.0)
        if j + 2 >= count:
            break
        u0 = (l0 * t - l1 * q) * inv
        u1 = (l1 * p - l0 * q) * inv
        v0 = (r0 * t - r1 * q) * inv
        v1 = (r1 * p - r0 * q) * inv
        for i in range(b, blocks):
            if i == b and s == 6:
                continue
            c0, c1 = full(left[i][:, j:j + 1]), full(left[i][:, j + 1:j + 2])
            if i == b:
                c0 = jnp.where(subs > s + 1, c0, 0.0)
                c1 = jnp.where(subs > s + 1, c1, 0.0)
            left[i] = left[i] - c0 * u0 - c1 * u1
            right[i] = right[i] - c0 * v0 - c1 * v1


def factor_x_kernel(rank_ref, sketch_ref, out_ref):
    sketch_t = sketch_ref[...]
    eliminate(exact(sketch_t, sketch_t, dims(1, 1)), sketch_t.shape[0], rank_ref[0], out_ref)


def inverse_factor_x(rank, sketch_t):
    width = sketch_t.shape[0]
    return pl.pallas_call(
        factor_x_kernel,
        in_specs=[pl.BlockSpec(memory_space=pltpu.SMEM)] + vmem(1),
        out_specs=pl.BlockSpec(memory_space=pltpu.VMEM),
        out_shape=jax.ShapeDtypeStruct((width, width), jnp.float32),
        name="factor_x",
    )(rank, sketch_t)


def factor_y_kernel(divisor, rank_ref, *refs):
    *part_refs, out_ref, inverse = refs
    sketch = part_refs[0][...]
    for ref in part_refs[1:]:
        sketch = sketch + ref[...]
    sketch = sketch / divisor
    eliminate(exact(sketch, sketch, dims(0, 0)), sketch.shape[1], rank_ref[0], inverse)
    out_ref[...] = exact(sketch, inverse[...], dims(1, 1))


def make_factor_y(rank, parts, divisor):
    rows, width = parts[0].shape
    return pl.pallas_call(
        functools.partial(factor_y_kernel, divisor),
        in_specs=[pl.BlockSpec(memory_space=pltpu.SMEM)] + vmem(len(parts)),
        out_specs=pl.BlockSpec(memory_space=pltpu.VMEM),
        out_shape=jax.ShapeDtypeStruct((rows, width), jnp.float32),
        scratch_shapes=[pltpu.VMEM((width, width), jnp.float32)],
        name="factor_y",
    )(rank, *parts)


def body(field, omega_x, omega_y, rank_x, rank_y):
    planes, rows_y, rows_z, cells_x = field.shape
    ranks_x = omega_x.shape[1]
    ranks_y = omega_y.shape[1]
    n_gy = lax.axis_size("gy")
    gy = lax.axis_index("gy")
    all_planes = planes * lax.axis_size("vert")
    all_rows_y = rows_y * n_gy
    all_rows_z = rows_z * lax.axis_size("gz")
    flat = field.reshape(-1, cells_x)

    sketch_t = sum_sketch(sketch_part(flat, omega_x)) / float(all_planes * all_rows_y * all_rows_z)

    share_z = rows_z // n_gy
    field_z = field.reshape(planes * rows_y, rows_z, cells_x)
    if share_z % 8 == 0:
        cut = lambda who: field_chunk(who[None].astype(jnp.int32), field_z, sketch_t, share_z)
    else:
        raw = lax.dot_general(flat, sketch_t, dims(1, 1), precision=HIGH)
        raw = raw.reshape(planes * rows_y, rows_z, ranks_x)
        cut = lambda who: lax.dynamic_slice_in_dim(raw, who * share_z, share_z, 1)
    chunks = [None] * n_gy
    for s in steps(n_gy):
        chunks[s] = swap(cut(gy ^ s), "gy", s)
    chunks[0] = cut(gy)

    inverse_x = inverse_factor_x(rank_x, sketch_t)
    factor_x = lax.dot_general(sketch_t, inverse_x, dims(0, 1), precision=HIGH)

    spread = jnp.stack(chunks).reshape(-1, ranks_x)
    spread = lax.dot_general(spread, inverse_x, dims(1, 1), precision=HIGH)
    spread = spread.reshape(n_gy, planes, rows_y, share_z, ranks_x)
    local_gram_y = jnp.einsum("gvazr,hvbzr->gahb", spread, spread, precision=HIGH)
    local_gram_y = local_gram_y.reshape(all_rows_y, all_rows_y)
    omega_p = by_step(omega_y.reshape(n_gy, rows_y, ranks_y), gy, n_gy).reshape(all_rows_y, ranks_y)
    part_y = jnp.dot(local_gram_y, omega_p, precision=HIGHEST)
    part_y = by_step(part_y.reshape(n_gy, rows_y, ranks_y), gy, n_gy).reshape(all_rows_y, ranks_y)
    for axis in ("vert", "gz"):
        count = lax.axis_size(axis)
        got = [swap(part_y, axis, s) for s in steps(count)]
        for other in got:
            part_y = part_y + other
    parts = [part_y] + [swap(part_y, "gy", s) for s in steps(n_gy)]
    factor_y = make_factor_y(rank_y, parts, float(all_planes * all_rows_z * ranks_x))

    share_k = ranks_y // n_gy
    weights = by_step(factor_y.reshape(n_gy, rows_y, ranks_y), gy, n_gy)
    weights = weights.reshape(n_gy, rows_y, n_gy, share_k)
    weights = jnp.moveaxis(by_step(jnp.moveaxis(weights, 2, 0), gy, n_gy), 0, 2)
    mixed = jnp.einsum("gvyzr,gyhk->hvkzr", spread, weights, precision=HIGH)
    pieces = [None] * n_gy
    for s in steps(n_gy):
        pieces[s] = swap(mixed[s], "gy", s)
    pieces[0] = mixed[0]
    core = by_step(jnp.stack(pieces), gy, n_gy)
    core = jnp.moveaxis(core, 0, 2).reshape(planes, share_k, rows_z, ranks_x)
    return (core, factor_x, factor_y)


def solution(mesh):
    in_specs = (P(("grp", "vert"), "gy", "gz", None), P(), P(), P("grp"), P("grp"))
    out_specs = (P(("grp", "vert"), "gy", "gz", None), P("grp", None), P("grp", None))
    return jax.shard_map(body, mesh=mesh, in_specs=in_specs, out_specs=out_specs, check_vma=False)
```

```python
import functools

import jax
import jax.numpy as jnp
from jax import lax
from jax.experimental import pallas as pl
from jax.experimental.pallas import tpu as pltpu
from jax.sharding import PartitionSpec as P

HIGH = lax.Precision.HIGH
HIGHEST = lax.Precision.HIGHEST


def swap(value, axes, step):
    count = lax.axis_size(axes)
    assert count & (count - 1) == 0
    return lax.ppermute(value, axes, [(i, i ^ step) for i in range(count)])


def steps(count):
    return sorted(range(1, count), key=lambda s: -(s & 2) * 4 - s)


def by_step(blocks, me, count):
    if count == 4:
        pairs = blocks.reshape((2, 2) + blocks.shape[1:])
        pairs = jnp.where(me & 2 != 0, pairs[::-1], pairs)
        pairs = jnp.where(me & 1 != 0, pairs[:, ::-1], pairs)
        return pairs.reshape(blocks.shape)
    return jnp.take(blocks, me ^ jnp.arange(count), axis=0)


def sum_over_gy(part):
    count = lax.axis_size("gy")
    got = [swap(part, "gy", s) for s in steps(count)]
    for other in got:
        part = part + other
    return part


def sum_sketch(parts, me):
    axes = ("gz", "vert")
    count = len(parts)
    got = [swap(parts[s], axes, s) for s in steps(count)]
    mine = parts[0]
    for other in got:
        mine = mine + other
    mine = sum_over_gy(mine)
    share, cells = mine.shape
    whole = jnp.zeros((share * count, cells), jnp.float32)
    whole = lax.dynamic_update_slice_in_dim(whole, mine, me * share, 0)
    got = [(s, swap(mine, axes, s)) for s in steps(count)]
    for s, other in got:
        whole = lax.dynamic_update_slice_in_dim(whole, other, (me ^ s) * share, 0)
    return whole


def dims(left, right):
    return (((left,), (right,)), ((), ()))


def mxu(a, b, numbers):
    return lax.dot_general(a, b, numbers, preferred_element_type=jnp.float32)


def exact(a, b, numbers):
    return lax.dot_general(a, b, numbers, precision=HIGHEST, preferred_element_type=jnp.float32)


def halves(value):
    high = value.astype(jnp.bfloat16)
    return high, (value - high.astype(jnp.float32)).astype(jnp.bfloat16)


VMEM = pl.BlockSpec(memory_space=pltpu.VMEM)
SMEM = pl.BlockSpec(memory_space=pltpu.SMEM)


def held(value):
    return pltpu.with_memory_space_constraint(value, pltpu.VMEM)


def kernel_call(body, name, out_shape, scalars, values, scratch=(), limit=16, whole_out=False):
    many = isinstance(out_shape, list)
    shapes = out_shape if many else [out_shape]
    if whole_out:
        outs = [jax.ShapeDtypeStruct(shape, jnp.float32) for shape in shapes]
    else:
        outs = [pltpu.VMEM(shape, jnp.float32) for shape in shapes]
    return pl.pallas_call(
        body,
        in_specs=[SMEM] * len(scalars) + [VMEM] * len(values),
        out_specs=[VMEM] * len(outs) if many else VMEM,
        out_shape=outs if many else outs[0],
        scratch_shapes=list(scratch),
        compiler_params=pltpu.CompilerParams(vmem_limit_bytes=limit << 20),
        name=name,
    )(*scalars, *[held(value) for value in values])


PIECES = 4


def sketch_kernel(me_ref, field_hbm, omega_ref, field_ref, *refs):
    *part_refs, total, arrived = refs
    width = omega_ref.shape[1]
    block = field_ref.shape[0] // PIECES
    copies = []
    for i in range(PIECES):
        rows = pl.ds(i * block, block)
        copies.append(pltpu.make_async_copy(field_hbm.at[rows], field_ref.at[rows], arrived.at[i]))
        copies[i].start()
    omega_high, omega_low = halves(omega_ref[...])
    omega_both = jnp.concatenate([omega_high, omega_low], axis=1)
    wide = narrow = None
    for i in range(PIECES):
        copies[i].wait()
        high, low = halves(field_ref[i * block:(i + 1) * block, :])
        both = mxu(high, omega_both, dims(1, 0))
        projected = both[:, :width] + (both[:, width:] + mxu(low, omega_high, dims(1, 0)))
        proj_high, proj_low = halves(projected)
        first = mxu(jnp.concatenate([proj_high, proj_low], axis=1), high, dims(0, 0))
        second = mxu(proj_high, low, dims(0, 0))
        wide = first if wide is None else wide + first
        narrow = second if narrow is None else narrow + second
    total[...] = wide[:width, :] + (wide[width:, :] + narrow)
    share = width // len(part_refs)
    for k, ref in enumerate(part_refs):
        start = pl.multiple_of((me_ref[0] ^ k) * share, share)
        ref[...] = total[pl.ds(start, share), :]


def sketch_parts(me, count, flat, omega):
    rows, cells = flat.shape
    width = omega.shape[1]
    out = pl.pallas_call(
        sketch_kernel,
        in_specs=[SMEM, pl.BlockSpec(memory_space=pltpu.HBM), VMEM],
        out_specs=[VMEM] * (1 + count),
        out_shape=[pltpu.VMEM((rows, cells), jnp.float32)]
        + [pltpu.VMEM((width // count, cells), jnp.float32)] * count,
        scratch_shapes=[pltpu.VMEM((width, cells), jnp.float32), pltpu.SemaphoreType.DMA((PIECES,))],
        compiler_params=pltpu.CompilerParams(vmem_limit_bytes=24 << 20),
        name="sketch",
    )(me, flat, held(omega))
    return out[0], out[1:]


def chunk_kernel(where_ref, field_ref, sketch_ref, out_ref):
    width, cells = sketch_ref.shape
    rows, share, _ = out_ref.shape
    start = pl.multiple_of(where_ref[0] * share, share)
    high, low = halves(field_ref[:, pl.ds(start, share), :].reshape(rows * share, cells))
    sketch_high, sketch_low = halves(sketch_ref[...])
    both = mxu(high, jnp.concatenate([sketch_high, sketch_low], axis=0), dims(1, 1))
    raw = both[:, :width] + (both[:, width:] + mxu(low, sketch_high, dims(1, 1)))
    out_ref[...] = raw.reshape(rows, share, width)


def field_chunk(where, field, sketch_t, share):
    shape = (field.shape[0], share, sketch_t.shape[0])
    return kernel_call(chunk_kernel, "chunk", shape, [where], [field, sketch_t])


def gram_kernel(planes, me_ref, inverse_ref, omega_ref, *refs):
    *chunk_refs, spread_ref, part_ref = refs
    rows, share, width = chunk_refs[0].shape
    rows_y = rows // planes
    inv_high, inv_low = halves(inverse_ref[...])
    inv_both = jnp.concatenate([inv_high, inv_low], axis=0)
    slabs, weights = [], []
    for k, ref in enumerate(chunk_refs):
        high, low = halves(ref[...].reshape(rows * share, width))
        both = mxu(high, inv_both, dims(1, 1))
        value = both[:, :width] + (both[:, width:] + mxu(low, inv_high, dims(1, 1)))
        value = jnp.swapaxes(value.reshape(planes, rows_y, share, width), 1, 2)
        slabs.append(jnp.concatenate([value[v, z] for v in range(planes) for z in range(share)], axis=1))
        start = pl.multiple_of((me_ref[0] ^ k) * rows_y, rows_y)
        weights.append(omega_ref[pl.ds(start, rows_y), :])
    spread = jnp.concatenate(slabs, axis=0)
    spread_ref[...] = spread
    high, low = halves(spread)
    gram = mxu(high, high, dims(1, 1)) + (mxu(high, low, dims(1, 1)) + mxu(low, high, dims(1, 1)))
    part = exact(gram, jnp.concatenate(weights, axis=0), dims(1, 0))
    for k in range(len(chunk_refs)):
        start = pl.multiple_of((me_ref[0] ^ k) * rows_y, rows_y)
        part_ref[pl.ds(start, rows_y), :] = part[k * rows_y:(k + 1) * rows_y, :]


def mix_kernel(me_ref, factor_ref, spread_ref, *refs):
    *out_refs, mixed = refs
    planes, share_k, share_z, width = out_refs[0].shape
    count = len(out_refs)
    rows_y = factor_ref.shape[0] // count
    own = [factor_ref[pl.ds(pl.multiple_of((me_ref[0] ^ k) * rows_y, rows_y), rows_y), :] for k in range(count)]
    fac_high, fac_low = halves(jnp.concatenate(own, axis=0))
    high, low = halves(spread_ref[...])
    mixed[...] = mxu(fac_high, high, dims(0, 0)) + (mxu(fac_high, low, dims(0, 0)) + mxu(fac_low, high, dims(0, 0)))
    for k, ref in enumerate(out_refs):
        start = pl.multiple_of((me_ref[0] ^ k) * share_k, share_k)
        block = mixed[pl.ds(start, share_k), :]
        for v in range(planes):
            at = lambda z: (v * share_z + z) * width
            rows = jnp.stack([block[:, at(z):at(z) + width] for z in range(share_z)], axis=0)
            ref[v] = jnp.swapaxes(rows, 0, 1)


def place_kernel(me_ref, *refs):
    *piece_refs, out_ref = refs
    share = piece_refs[0].shape[2]
    for k, ref in enumerate(piece_refs):
        start = pl.multiple_of((me_ref[0] ^ k) * share, share)
        out_ref[:, :, pl.ds(start, share), :] = ref[...]


def eliminate(gram, count, rank, out_ref):
    lanes = lax.broadcasted_iota(jnp.int32, (8, count), 1)
    subs = lax.broadcasted_iota(jnp.int32, (8, count), 0)
    blocks = count // 8
    full = lambda x: jnp.broadcast_to(x, (8, count))
    left = [gram[8 * b:8 * b + 8, :] for b in range(blocks)]
    right = [(lanes == subs + 8 * b).astype(jnp.float32) for b in range(blocks)]
    for j in range(0, count, 2):
        b, s = divmod(j, 8)
        l0, l1 = full(left[b][s:s + 1, :]), full(left[b][s + 1:s + 2, :])
        r0, r1 = full(right[b][s:s + 1, :]), full(right[b][s + 1:s + 2, :])
        p, q, t = full(l0[:, j:j + 1]), full(l0[:, j + 1:j + 2]), full(l1[:, j + 1:j + 2])
        inv = 1.0 / (p * t - q * q)
        ratio = q / p
        first = r0 * lax.rsqrt(p)
        second = (r1 - ratio * r0) * lax.rsqrt(t - q * ratio)
        out_ref[j:j + 1, :] = jnp.where(j < rank, first[0:1], 0.0)
        out_ref[j + 1:j + 2, :] = jnp.where(j + 1 < rank, second[0:1], 0.0)
        if j + 2 >= count:
            break
        u0 = (l0 * t - l1 * q) * inv
        u1 = (l1 * p - l0 * q) * inv
        v0 = (r0 * t - r1 * q) * inv
        v1 = (r1 * p - r0 * q) * inv
        for i in range(b, blocks):
            if i == b and s == 6:
                continue
            c0, c1 = full(left[i][:, j:j + 1]), full(left[i][:, j + 1:j + 2])
            if i == b:
                c0 = jnp.where(subs > s + 1, c0, 0.0)
                c1 = jnp.where(subs > s + 1, c1, 0.0)
            left[i] = left[i] - c0 * u0 - c1 * u1
            right[i] = right[i] - c0 * v0 - c1 * v1


def factor_x_kernel(rank_ref, sketch_ref, out_ref):
    sketch_t = sketch_ref[...]
    eliminate(exact(sketch_t, sketch_t, dims(1, 1)), sketch_t.shape[0], rank_ref[0], out_ref)


def inverse_factor_x(rank, sketch_t):
    width = sketch_t.shape[0]
    return kernel_call(factor_x_kernel, "factor_x", (width, width), [rank], [sketch_t])


def factor_y_kernel(divisor, rank_ref, *refs):
    *part_refs, out_ref, inverse = refs
    sketch = part_refs[0][...]
    for ref in part_refs[1:]:
        sketch = sketch + ref[...]
    sketch = sketch / divisor
    eliminate(exact(sketch, sketch, dims(0, 0)), sketch.shape[1], rank_ref[0], inverse)
    out_ref[...] = exact(sketch, inverse[...], dims(1, 1))


def make_factor_y(rank, parts, divisor):
    width = parts[0].shape[1]
    scratch = [pltpu.VMEM((width, width), jnp.float32)]
    kernel = functools.partial(factor_y_kernel, divisor)
    return kernel_call(kernel, "factor_y", parts[0].shape, [rank], parts, scratch)


def body(field, omega_x, omega_y, rank_x, rank_y):
    planes, rows_y, rows_z, cells_x = field.shape
    ranks_x = omega_x.shape[1]
    ranks_y = omega_y.shape[1]
    n_gy = lax.axis_size("gy")
    gy = lax.axis_index("gy")
    all_planes = planes * lax.axis_size("vert")
    all_rows_y = rows_y * n_gy
    all_rows_z = rows_z * lax.axis_size("gz")
    flat = field.reshape(-1, cells_x)

    here = gy[None].astype(jnp.int32)
    quarter = lax.axis_index("gz") * lax.axis_size("vert") + lax.axis_index("vert")
    n_quarter = lax.axis_size(("gz", "vert"))
    field_v, parts = sketch_parts(quarter[None].astype(jnp.int32), n_quarter, flat, omega_x)
    sketch_t = sum_sketch(parts, quarter) / float(all_planes * all_rows_y * all_rows_z)

    share_z = rows_z // n_gy
    share_k = ranks_y // n_gy
    field_z = field_v.reshape(planes * rows_y, rows_z, cells_x)
    tiled = share_z % 8 == 0 and share_k % 8 == 0
    if tiled:
        cut = lambda who: field_chunk(who[None].astype(jnp.int32), field_z, sketch_t, share_z)
    else:
        raw = lax.dot_general(flat, sketch_t, dims(1, 1), precision=HIGH)
        raw = raw.reshape(planes * rows_y, rows_z, ranks_x)
        cut = lambda who: lax.dynamic_slice_in_dim(raw, who * share_z, share_z, 1)
    chunks = [None] * n_gy
    for s in steps(n_gy):
        chunks[s] = swap(cut(gy ^ s), "gy", s)
    chunks[0] = cut(gy)

    inverse_x = inverse_factor_x(rank_x, sketch_t)
    factor_x = lax.dot_general(sketch_t, inverse_x, dims(0, 1), precision=HIGH)

    if tiled:
        samples = planes * share_z * ranks_x
        spread, part_y = kernel_call(
            functools.partial(gram_kernel, planes),
            "gram",
            [(all_rows_y, samples), (all_rows_y, ranks_y)],
            [here],
            [inverse_x, omega_y] + chunks,
        )
    else:
        spread = jnp.stack(chunks).reshape(-1, ranks_x)
        spread = lax.dot_general(spread, inverse_x, dims(1, 1), precision=HIGH)
        spread = spread.reshape(n_gy, planes, rows_y, share_z, ranks_x)
        local_gram_y = jnp.einsum("gvazr,hvbzr->gahb", spread, spread, precision=HIGH)
        local_gram_y = local_gram_y.reshape(all_rows_y, all_rows_y)
        omega_p = by_step(omega_y.reshape(n_gy, rows_y, ranks_y), gy, n_gy).reshape(all_rows_y, ranks_y)
        part_y = jnp.dot(local_gram_y, omega_p, precision=HIGHEST)
        part_y = by_step(part_y.reshape(n_gy, rows_y, ranks_y), gy, n_gy).reshape(all_rows_y, ranks_y)
    for axis in ("vert", "gz"):
        count = lax.axis_size(axis)
        got = [swap(part_y, axis, s) for s in steps(count)]
        for other in got:
            part_y = part_y + other
    parts = [part_y] + [swap(part_y, "gy", s) for s in steps(n_gy)]
    factor_y = make_factor_y(rank_y, parts, float(all_planes * all_rows_z * ranks_x))

    if tiled:
        shape = (planes, share_k, share_z, ranks_x)
        scratch = [pltpu.VMEM((ranks_y, spread.shape[1]), jnp.float32)]
        mixed = kernel_call(mix_kernel, "mix", [shape] * n_gy, [here], [factor_y, spread], scratch)
        pieces = [mixed[0]] + [None] * (n_gy - 1)
        for s in steps(n_gy):
            pieces[s] = swap(mixed[s], "gy", s)
        shape = (planes, share_k, rows_z, ranks_x)
        core = kernel_call(place_kernel, "place", shape, [here], pieces, whole_out=True)
        return (core, factor_x, factor_y)
    weights = by_step(factor_y.reshape(n_gy, rows_y, ranks_y), gy, n_gy)
    weights = weights.reshape(n_gy, rows_y, n_gy, share_k)
    weights = jnp.moveaxis(by_step(jnp.moveaxis(weights, 2, 0), gy, n_gy), 0, 2)
    mixed = jnp.einsum("gvyzr,gyhk->hvkzr", spread, weights, precision=HIGH)
    pieces = [None] * n_gy
    for s in steps(n_gy):
        pieces[s] = swap(mixed[s], "gy", s)
    pieces[0] = mixed[0]
    core = by_step(jnp.stack(pieces), gy, n_gy)
    core = jnp.moveaxis(core, 0, 2).reshape(planes, share_k, rows_z, ranks_x)
    return (core, factor_x, factor_y)


def solution(mesh):
    in_specs = (P(("grp", "vert"), "gy", "gz", None), P(), P(), P("grp"), P("grp"))
    out_specs = (P(("grp", "vert"), "gy", "gz", None), P("grp", None), P("grp", None))
    return jax.shard_map(body, mesh=mesh, in_specs=in_specs, out_specs=out_specs, check_vma=False)
```

```python
import functools

import jax
import jax.numpy as jnp
from jax import lax
from jax.experimental import pallas as pl
from jax.experimental.pallas import tpu as pltpu
from jax.sharding import PartitionSpec as P

HIGH = lax.Precision.HIGH
HIGHEST = lax.Precision.HIGHEST


def swap(value, axes, step):
    count = lax.axis_size(axes)
    assert count & (count - 1) == 0
    return lax.ppermute(value, axes, [(i, i ^ step) for i in range(count)])


def steps(count):
    return sorted(range(1, count), key=lambda s: -(s & 2) * 4 - s)


def by_step(blocks, me, count):
    if count == 4:
        pairs = blocks.reshape((2, 2) + blocks.shape[1:])
        pairs = jnp.where(me & 2 != 0, pairs[::-1], pairs)
        pairs = jnp.where(me & 1 != 0, pairs[:, ::-1], pairs)
        return pairs.reshape(blocks.shape)
    return jnp.take(blocks, me ^ jnp.arange(count), axis=0)


def sum_over_gy(part):
    count = lax.axis_size("gy")
    got = [swap(part, "gy", s) for s in steps(count)]
    for other in got:
        part = part + other
    return part


def sum_sketch(parts):
    axes = ("gz", "vert")
    count = len(parts)
    got = [swap(parts[s], axes, s) for s in steps(count)]
    mine = parts[0]
    for other in got:
        mine = mine + other
    mine = sum_over_gy(mine)
    pieces = [mine] + [None] * (count - 1)
    for s in steps(count):
        pieces[s] = swap(mine, axes, s)
    return pieces


def dims(left, right):
    return (((left,), (right,)), ((), ()))


def mxu(a, b, numbers):
    return lax.dot_general(a, b, numbers, preferred_element_type=jnp.float32)


def exact(a, b, numbers):
    return lax.dot_general(a, b, numbers, precision=HIGHEST, preferred_element_type=jnp.float32)


def halves(value):
    high = value.astype(jnp.bfloat16)
    return high, (value - high.astype(jnp.float32)).astype(jnp.bfloat16)


VMEM = pl.BlockSpec(memory_space=pltpu.VMEM)
SMEM = pl.BlockSpec(memory_space=pltpu.SMEM)


def held(value):
    return pltpu.with_memory_space_constraint(value, pltpu.VMEM)


def kernel_call(body, name, out_shape, scalars, values, scratch=(), limit=16, whole_out=False):
    many = isinstance(out_shape, list)
    shapes = out_shape if many else [out_shape]
    if whole_out:
        outs = [jax.ShapeDtypeStruct(shape, jnp.float32) for shape in shapes]
    else:
        outs = [pltpu.VMEM(shape, jnp.float32) for shape in shapes]
    return pl.pallas_call(
        body,
        in_specs=[SMEM] * len(scalars) + [VMEM] * len(values),
        out_specs=[VMEM] * len(outs) if many else VMEM,
        out_shape=outs if many else outs[0],
        scratch_shapes=list(scratch),
        compiler_params=pltpu.CompilerParams(vmem_limit_bytes=limit << 20),
        name=name,
    )(*scalars, *[held(value) for value in values])


PIECES = 4


def sketch_kernel(me_ref, here_ref, field_hbm, omega_hbm, field_ref, *refs):
    *part_refs, omega_ref, total, arrived = refs
    omega_copy = pltpu.make_async_copy(omega_hbm, omega_ref, arrived.at[PIECES])
    omega_copy.start()
    width = omega_ref.shape[1]
    block = field_ref.shape[0] // PIECES
    copies = []
    for i in range(PIECES):
        rows = pl.ds(i * block, block)
        copies.append(pltpu.make_async_copy(field_hbm.at[rows], field_ref.at[rows], arrived.at[i]))
        copies[i].start()
    omega_copy.wait()
    omega_high, omega_low = halves(omega_ref[...])
    omega_both = jnp.concatenate([omega_high, omega_low], axis=1)
    wide = narrow = None
    for i in range(PIECES):
        copies[i].wait()
        high, low = halves(field_ref[i * block:(i + 1) * block, :])
        both = mxu(high, omega_both, dims(1, 0))
        projected = both[:, :width] + (both[:, width:] + mxu(low, omega_high, dims(1, 0)))
        proj_high, proj_low = halves(projected)
        first = mxu(jnp.concatenate([proj_high, proj_low], axis=1), high, dims(0, 0))
        second = mxu(proj_high, low, dims(0, 0))
        wide = first if wide is None else wide + first
        narrow = second if narrow is None else narrow + second
    total[...] = wide[:width, :] + (wide[width:, :] + narrow)
    share = width // len(part_refs)
    for k, ref in enumerate(part_refs):
        start = pl.multiple_of((me_ref[0] ^ k) * share, share)
        ref[...] = total[pl.ds(start, share), :]


def sketch_parts(me, here, count, flat, omega):
    rows, cells = flat.shape
    width = omega.shape[1]
    far = pl.BlockSpec(memory_space=pltpu.HBM)
    out = pl.pallas_call(
        sketch_kernel,
        in_specs=[SMEM, SMEM, far, far],
        out_specs=[VMEM] * (1 + count),
        out_shape=[pltpu.VMEM((rows, cells), jnp.float32)]
        + [pltpu.VMEM((width // count, cells), jnp.float32)] * count,
        scratch_shapes=[
            pltpu.VMEM((cells, width), jnp.float32),
            pltpu.VMEM((width, cells), jnp.float32),
            pltpu.SemaphoreType.DMA((PIECES + 1,)),
        ],
        compiler_params=pltpu.CompilerParams(vmem_limit_bytes=24 << 20),
        name="sketch",
    )(me, here, *[pltpu.with_memory_space_constraint(x, pltpu.HBM) for x in (flat, omega)])
    return out[0], out[1:]


def gather_sketch(scale, me_ref, piece_refs, whole):
    share = piece_refs[0].shape[0]
    for k, ref in enumerate(piece_refs):
        start = pl.multiple_of((me_ref[0] ^ k) * share, share)
        whole[pl.ds(start, share), :] = ref[...] * scale
    return whole[...]


def chunk_kernel(scale, step, me_ref, here_ref, field_ref, *refs):
    *piece_refs, out_ref, whole = refs
    sketch = gather_sketch(scale, me_ref, piece_refs, whole)
    width, cells = sketch.shape
    rows, share, _ = out_ref.shape
    start = pl.multiple_of((here_ref[0] ^ step) * share, share)
    high, low = halves(field_ref[:, pl.ds(start, share), :].reshape(rows * share, cells))
    sketch_high, sketch_low = halves(sketch)
    both = mxu(high, jnp.concatenate([sketch_high, sketch_low], axis=0), dims(1, 1))
    raw = both[:, :width] + (both[:, width:] + mxu(low, sketch_high, dims(1, 1)))
    out_ref[...] = raw.reshape(rows, share, width)


def field_chunk(scale, step, places, field, pieces, share):
    width, cells = pieces[0].shape[0] * len(pieces), field.shape[2]
    scratch = [pltpu.VMEM((width, cells), jnp.float32)]
    kernel = functools.partial(chunk_kernel, scale, step)
    return kernel_call(kernel, "chunk", (field.shape[0], share, width), places, [field] + pieces, scratch)


def gram_kernel(planes, me_ref, inverse_ref, omega_ref, *refs):
    *chunk_refs, spread_ref, part_ref = refs
    rows, share, width = chunk_refs[0].shape
    rows_y = rows // planes
    inv_high, inv_low = halves(inverse_ref[...])
    inv_both = jnp.concatenate([inv_high, inv_low], axis=0)
    for k, ref in enumerate(chunk_refs):
        high, low = halves(ref[...].reshape(rows * share, width))
        both = mxu(high, inv_both, dims(1, 1))
        value = both[:, :width] + (both[:, width:] + mxu(low, inv_high, dims(1, 1)))
        value = jnp.swapaxes(value.reshape(planes, rows_y, share, width), 1, 2)
        start = pl.multiple_of((me_ref[0] ^ k) * rows_y, rows_y)
        slab = jnp.concatenate([value[v, z] for v in range(planes) for z in range(share)], axis=1)
        spread_ref[pl.ds(start, rows_y), :] = slab
    high, low = halves(spread_ref[...])
    gram = mxu(high, high, dims(1, 1)) + (mxu(high, low, dims(1, 1)) + mxu(low, high, dims(1, 1)))
    part_ref[...] = exact(gram, omega_ref[...], dims(1, 1))


def mix_kernel(me_ref, factor_ref, spread_ref, *refs):
    *out_refs, mixed = refs
    planes, share_k, share_z, width = out_refs[0].shape
    fac_high, fac_low = halves(factor_ref[...])
    high, low = halves(spread_ref[...])
    mixed[...] = mxu(fac_high, high, dims(0, 0)) + (mxu(fac_high, low, dims(0, 0)) + mxu(fac_low, high, dims(0, 0)))
    for k, ref in enumerate(out_refs):
        start = pl.multiple_of((me_ref[0] ^ k) * share_k, share_k)
        block = mixed[pl.ds(start, share_k), :]
        for v in range(planes):
            at = lambda z: (v * share_z + z) * width
            rows = jnp.stack([block[:, at(z):at(z) + width] for z in range(share_z)], axis=0)
            ref[v] = jnp.swapaxes(rows, 0, 1)


def place_kernel(me_ref, *refs):
    *piece_refs, out_ref = refs
    share = piece_refs[0].shape[2]
    for k, ref in enumerate(piece_refs):
        start = pl.multiple_of((me_ref[0] ^ k) * share, share)
        out_ref[:, :, pl.ds(start, share), :] = ref[...]


def eliminate(gram, count, rank, out_ref):
    lanes = lax.broadcasted_iota(jnp.int32, (8, count), 1)
    subs = lax.broadcasted_iota(jnp.int32, (8, count), 0)
    blocks = count // 8
    full = lambda x: jnp.broadcast_to(x, (8, count))
    left = [gram[8 * b:8 * b + 8, :] for b in range(blocks)]
    right = [(lanes == subs + 8 * b).astype(jnp.float32) for b in range(blocks)]
    for j in range(0, count, 2):
        b, s = divmod(j, 8)
        l0, l1 = full(left[b][s:s + 1, :]), full(left[b][s + 1:s + 2, :])
        r0, r1 = full(right[b][s:s + 1, :]), full(right[b][s + 1:s + 2, :])
        p, q, t = full(l0[:, j:j + 1]), full(l0[:, j + 1:j + 2]), full(l1[:, j + 1:j + 2])
        inv = 1.0 / (p * t - q * q)
        ratio = q / p
        first = r0 * lax.rsqrt(p)
        second = (r1 - ratio * r0) * lax.rsqrt(t - q * ratio)
        out_ref[j:j + 1, :] = jnp.where(j < rank, first[0:1], 0.0)
        out_ref[j + 1:j + 2, :] = jnp.where(j + 1 < rank, second[0:1], 0.0)
        if j + 2 >= count:
            break
        u0 = (l0 * t - l1 * q) * inv
        u1 = (l1 * p - l0 * q) * inv
        v0 = (r0 * t - r1 * q) * inv
        v1 = (r1 * p - r0 * q) * inv
        for i in range(b, blocks):
            if i == b and s == 6:
                continue
            c0, c1 = full(left[i][:, j:j + 1]), full(left[i][:, j + 1:j + 2])
            if i == b:
                c0 = jnp.where(subs > s + 1, c0, 0.0)
                c1 = jnp.where(subs > s + 1, c1, 0.0)
            left[i] = left[i] - c0 * u0 - c1 * u1
            right[i] = right[i] - c0 * v0 - c1 * v1


def factor_x_kernel(scale, rank_ref, me_ref, *refs):
    *piece_refs, out_ref, sketch_ref = refs
    sketch_t = gather_sketch(scale, me_ref, piece_refs, sketch_ref)
    eliminate(exact(sketch_t, sketch_t, dims(1, 1)), sketch_t.shape[0], rank_ref[0], out_ref)


def inverse_factor_x(scale, rank, me, pieces):
    width = pieces[0].shape[0] * len(pieces)
    scratch = [pltpu.VMEM((width, pieces[0].shape[1]), jnp.float32)]
    kernel = functools.partial(factor_x_kernel, scale)
    return kernel_call(kernel, "factor_x", (width, width), [rank, me], pieces, scratch)


def apply_kernel(scale, me_ref, inverse_ref, *refs):
    *piece_refs, out_ref, whole = refs
    sketch_t = gather_sketch(scale, me_ref, piece_refs, whole)
    out_ref[...] = exact(sketch_t, inverse_ref[...], dims(0, 1))


def make_factor_x(scale, me, inverse, pieces):
    width, cells = inverse.shape[0], pieces[0].shape[1]
    scratch = [pltpu.VMEM((width, cells), jnp.float32)]
    kernel = functools.partial(apply_kernel, scale)
    return kernel_call(kernel, "apply", (cells, width), [me], [inverse] + pieces, scratch, whole_out=True)


def factor_y_kernel(divisor, rank_ref, *refs):
    *part_refs, out_ref, inverse = refs
    sketch = part_refs[0][...]
    for ref in part_refs[1:]:
        sketch = sketch + ref[...]
    sketch = sketch / divisor
    eliminate(exact(sketch, sketch, dims(0, 0)), sketch.shape[1], rank_ref[0], inverse)
    out_ref[...] = exact(sketch, inverse[...], dims(1, 1))


def make_factor_y(rank, parts, divisor):
    width = parts[0].shape[1]
    scratch = [pltpu.VMEM((width, width), jnp.float32)]
    kernel = functools.partial(factor_y_kernel, divisor)
    return kernel_call(kernel, "factor_y", parts[0].shape, [rank], parts, scratch)


def body(field, omega_x, omega_y, rank_x, rank_y):
    planes, rows_y, rows_z, cells_x = field.shape
    ranks_x = omega_x.shape[1]
    ranks_y = omega_y.shape[1]
    n_gy = lax.axis_size("gy")
    gy = lax.axis_index("gy")
    all_planes = planes * lax.axis_size("vert")
    all_rows_y = rows_y * n_gy
    all_rows_z = rows_z * lax.axis_size("gz")
    flat = field.reshape(-1, cells_x)

    here = gy[None].astype(jnp.int32)
    quarter = lax.axis_index("gz") * lax.axis_size("vert") + lax.axis_index("vert")
    n_quarter = lax.axis_size(("gz", "vert"))
    quarter = quarter[None].astype(jnp.int32)
    field_v, parts = sketch_parts(quarter, here, n_quarter, flat, omega_x)
    pieces = sum_sketch(parts)
    scale = 1.0 / float(all_planes * all_rows_y * all_rows_z)

    share_z = rows_z // n_gy
    share_k = ranks_y // n_gy
    field_z = field_v.reshape(planes * rows_y, rows_z, cells_x)
    tiled = share_z % 8 == 0 and share_k % 8 == 0
    if tiled:
        cut = lambda s: field_chunk(scale, s, [quarter, here], field_z, pieces, share_z)
    else:
        sketch_t = jnp.take(jnp.stack(pieces), quarter ^ jnp.arange(n_quarter), axis=0)
        sketch_t = sketch_t.reshape(ranks_x, cells_x) * scale
        raw = lax.dot_general(flat, sketch_t, dims(1, 1), precision=HIGH)
        raw = raw.reshape(planes * rows_y, rows_z, ranks_x)
        cut = lambda s: lax.dynamic_slice_in_dim(raw, (gy ^ s) * share_z, share_z, 1)
    chunks = [None] * n_gy
    for s in steps(n_gy):
        chunks[s] = swap(cut(s), "gy", s)
    chunks[0] = cut(0)

    inverse_x = inverse_factor_x(scale, rank_x, quarter, pieces)
    factor_x = make_factor_x(scale, quarter, inverse_x, pieces)

    if tiled:
        samples = planes * share_z * ranks_x
        spread, part_y = kernel_call(
            functools.partial(gram_kernel, planes),
            "gram",
            [(all_rows_y, samples), (all_rows_y, ranks_y)],
            [here],
            [inverse_x, omega_y.T] + chunks,
        )
    else:
        spread = jnp.stack(chunks).reshape(-1, ranks_x)
        spread = lax.dot_general(spread, inverse_x, dims(1, 1), precision=HIGH)
        spread = spread.reshape(n_gy, planes, rows_y, share_z, ranks_x)
        local_gram_y = jnp.einsum("gvazr,hvbzr->gahb", spread, spread, precision=HIGH)
        local_gram_y = local_gram_y.reshape(all_rows_y, all_rows_y)
        omega_p = by_step(omega_y.reshape(n_gy, rows_y, ranks_y), gy, n_gy).reshape(all_rows_y, ranks_y)
        part_y = jnp.dot(local_gram_y, omega_p, precision=HIGHEST)
        part_y = by_step(part_y.reshape(n_gy, rows_y, ranks_y), gy, n_gy).reshape(all_rows_y, ranks_y)
    for axis in ("vert", "gz"):
        count = lax.axis_size(axis)
        got = [swap(part_y, axis, s) for s in steps(count)]
        for other in got:
            part_y = part_y + other
    parts = [part_y] + [swap(part_y, "gy", s) for s in steps(n_gy)]
    factor_y = make_factor_y(rank_y, parts, float(all_planes * all_rows_z * ranks_x))

    if tiled:
        shape = (planes, share_k, share_z, ranks_x)
        scratch = [pltpu.VMEM((ranks_y, spread.shape[1]), jnp.float32)]
        mixed = kernel_call(mix_kernel, "mix", [shape] * n_gy, [here], [factor_y, spread], scratch)
        pieces = [mixed[0]] + [None] * (n_gy - 1)
        for s in steps(n_gy):
            pieces[s] = swap(mixed[s], "gy", s)
        shape = (planes, share_k, rows_z, ranks_x)
        core = kernel_call(place_kernel, "place", shape, [here], pieces, whole_out=True)
        return (core, factor_x, factor_y)
    weights = by_step(factor_y.reshape(n_gy, rows_y, ranks_y), gy, n_gy)
    weights = weights.reshape(n_gy, rows_y, n_gy, share_k)
    weights = jnp.moveaxis(by_step(jnp.moveaxis(weights, 2, 0), gy, n_gy), 0, 2)
    mixed = jnp.einsum("gvyzr,gyhk->hvkzr", spread, weights, precision=HIGH)
    pieces = [None] * n_gy
    for s in steps(n_gy):
        pieces[s] = swap(mixed[s], "gy", s)
    pieces[0] = mixed[0]
    core = by_step(jnp.stack(pieces), gy, n_gy)
    core = jnp.moveaxis(core, 0, 2).reshape(planes, share_k, rows_z, ranks_x)
    return (core, factor_x, factor_y)


def solution(mesh):
    in_specs = (P(("grp", "vert"), "gy", "gz", None), P(), P(), P("grp"), P("grp"))
    out_specs = (P(("grp", "vert"), "gy", "gz", None), P("grp", None), P("grp", None))
    return jax.shard_map(body, mesh=mesh, in_specs=in_specs, out_specs=out_specs, check_vma=False)
```

```python
import functools

import jax
import jax.numpy as jnp
from jax import lax
from jax.experimental import pallas as pl
from jax.experimental.pallas import tpu as pltpu
from jax.sharding import PartitionSpec as P

HIGH = lax.Precision.HIGH
HIGHEST = lax.Precision.HIGHEST


def swap(value, axes, step):
    count = lax.axis_size(axes)
    assert count & (count - 1) == 0
    return lax.ppermute(value, axes, [(i, i ^ step) for i in range(count)])


def steps(count):
    return sorted(range(1, count), key=lambda s: -(s & 2) * 4 - s)


def by_step(blocks, me, count):
    if count == 4:
        pairs = blocks.reshape((2, 2) + blocks.shape[1:])
        pairs = jnp.where(me & 2 != 0, pairs[::-1], pairs)
        pairs = jnp.where(me & 1 != 0, pairs[:, ::-1], pairs)
        return pairs.reshape(blocks.shape)
    return jnp.take(blocks, me ^ jnp.arange(count), axis=0)


def sum_over_gy(part):
    count = lax.axis_size("gy")
    got = [swap(part, "gy", s) for s in steps(count)]
    for other in got:
        part = part + other
    return part


def sum_sketch(parts):
    axes = ("gz", "vert")
    count = len(parts)
    got = [swap(parts[s], axes, s) for s in steps(count)]
    mine = parts[0]
    for other in got:
        mine = mine + other
    mine = sum_over_gy(mine)
    pieces = [mine] + [None] * (count - 1)
    for s in steps(count):
        pieces[s] = swap(mine, axes, s)
    return pieces


def dims(left, right):
    return (((left,), (right,)), ((), ()))


def mxu(a, b, numbers):
    return lax.dot_general(a, b, numbers, preferred_element_type=jnp.float32)


def exact(a, b, numbers):
    return lax.dot_general(a, b, numbers, precision=HIGHEST, preferred_element_type=jnp.float32)


def halves(value):
    high = value.astype(jnp.bfloat16)
    return high, (value - high.astype(jnp.float32)).astype(jnp.bfloat16)


VMEM = pl.BlockSpec(memory_space=pltpu.VMEM)
SMEM = pl.BlockSpec(memory_space=pltpu.SMEM)


def held(value):
    return pltpu.with_memory_space_constraint(value, pltpu.VMEM)


def kernel_call(body, name, out_shape, scalars, values, scratch=(), limit=16, whole_out=False):
    many = isinstance(out_shape, list)
    shapes = out_shape if many else [out_shape]
    if whole_out:
        outs = [jax.ShapeDtypeStruct(shape, jnp.float32) for shape in shapes]
    else:
        outs = [pltpu.VMEM(shape, jnp.float32) for shape in shapes]
    return pl.pallas_call(
        body,
        in_specs=[SMEM] * len(scalars) + [VMEM] * len(values),
        out_specs=[VMEM] * len(outs) if many else VMEM,
        out_shape=outs if many else outs[0],
        scratch_shapes=list(scratch),
        compiler_params=pltpu.CompilerParams(vmem_limit_bytes=limit << 20),
        name=name,
    )(*scalars, *[held(value) for value in values])


PIECES = 4


def sketch_kernel(me_ref, here_ref, field_hbm, omega_hbm, field_ref, *refs):
    *part_refs, omega_ref, total, arrived = refs
    omega_copy = pltpu.make_async_copy(omega_hbm, omega_ref, arrived.at[PIECES])
    omega_copy.start()
    width = omega_ref.shape[1]
    block = field_ref.shape[0] // PIECES
    copies = []
    for i in range(PIECES):
        rows = pl.ds(i * block, block)
        copies.append(pltpu.make_async_copy(field_hbm.at[rows], field_ref.at[rows], arrived.at[i]))
        copies[i].start()
    omega_copy.wait()
    omega_high, omega_low = halves(omega_ref[...])
    omega_both = jnp.concatenate([omega_high, omega_low], axis=1)
    wide = narrow = None
    for i in range(PIECES):
        copies[i].wait()
        high, low = halves(field_ref[i * block:(i + 1) * block, :])
        both = mxu(high, omega_both, dims(1, 0))
        projected = both[:, :width] + (both[:, width:] + mxu(low, omega_high, dims(1, 0)))
        proj_high, proj_low = halves(projected)
        first = mxu(jnp.concatenate([proj_high, proj_low], axis=1), high, dims(0, 0))
        second = mxu(proj_high, low, dims(0, 0))
        wide = first if wide is None else wide + first
        narrow = second if narrow is None else narrow + second
    total[...] = wide[:width, :] + (wide[width:, :] + narrow)
    share = width // len(part_refs)
    for k, ref in enumerate(part_refs):
        start = pl.multiple_of((me_ref[0] ^ k) * share, share)
        ref[...] = total[pl.ds(start, share), :]


def sketch_parts(me, here, count, flat, omega):
    rows, cells = flat.shape
    width = omega.shape[1]
    far = pl.BlockSpec(memory_space=pltpu.HBM)
    out = pl.pallas_call(
        sketch_kernel,
        in_specs=[SMEM, SMEM, far, far],
        out_specs=[VMEM] * (1 + count),
        out_shape=[pltpu.VMEM((rows, cells), jnp.float32)]
        + [pltpu.VMEM((width // count, cells), jnp.float32)] * count,
        scratch_shapes=[
            pltpu.VMEM((cells, width), jnp.float32),
            pltpu.VMEM((width, cells), jnp.float32),
            pltpu.SemaphoreType.DMA((PIECES + 1,)),
        ],
        compiler_params=pltpu.CompilerParams(vmem_limit_bytes=24 << 20),
        name="sketch",
    )(me, here, *[pltpu.with_memory_space_constraint(x, pltpu.HBM) for x in (flat, omega)])
    return out[0], out[1:]


def gather_sketch(scale, me_ref, piece_refs, whole):
    share = piece_refs[0].shape[0]
    for k, ref in enumerate(piece_refs):
        start = pl.multiple_of((me_ref[0] ^ k) * share, share)
        whole[pl.ds(start, share), :] = ref[...] * scale
    return whole[...]


def chunk_kernel(scale, step, me_ref, here_ref, field_ref, *refs):
    *piece_refs, _, out_ref, whole = refs
    sketch = gather_sketch(scale, me_ref, piece_refs, whole)
    width, cells = sketch.shape
    rows, share, _ = out_ref.shape
    start = pl.multiple_of((here_ref[0] ^ step) * share, share)
    high, low = halves(field_ref[:, pl.ds(start, share), :].reshape(rows * share, cells))
    sketch_high, sketch_low = halves(sketch)
    both = mxu(high, jnp.concatenate([sketch_high, sketch_low], axis=0), dims(1, 1))
    raw = both[:, :width] + (both[:, width:] + mxu(low, sketch_high, dims(1, 1)))
    out_ref[...] = raw.reshape(rows, share, width)


def field_chunk(scale, step, places, field, pieces, share, after):
    width, cells = pieces[0].shape[0] * len(pieces), field.shape[2]
    scratch = [pltpu.VMEM((width, cells), jnp.float32)]
    kernel = functools.partial(chunk_kernel, scale, step)
    shape = (field.shape[0], share, width)
    return kernel_call(kernel, "chunk", shape, places, [field] + pieces + [after], scratch)


def lift_kernel(planes, inverse_ref, chunk_ref, *refs):
    out_ref = refs[-1]
    rows, share, width = chunk_ref.shape
    inv_high, inv_low = halves(inverse_ref[...])
    high, low = halves(chunk_ref[...].reshape(rows * share, width))
    both = mxu(high, jnp.concatenate([inv_high, inv_low], axis=0), dims(1, 1))
    value = both[:, :width] + (both[:, width:] + mxu(low, inv_high, dims(1, 1)))
    value = jnp.swapaxes(value.reshape(planes, rows // planes, share, width), 1, 2)
    for v in range(planes):
        for z in range(share):
            at = (v * share + z) * width
            out_ref[:, at:at + width] = value[v, z]


def lift(planes, inverse, chunk, after):
    rows, share, width = chunk.shape
    shape = (rows // planes, planes * share * width)
    return kernel_call(functools.partial(lift_kernel, planes), "lift", shape, [], [inverse, chunk] + after)


def gram_kernel(me_ref, omega_ref, *refs):
    *slab_refs, part_ref, rows_ref, cols_ref = refs
    share = slab_refs[0].shape[0]
    high, low = halves(jnp.concatenate([ref[...] for ref in slab_refs], axis=0))
    rows_ref[...] = mxu(high, high, dims(1, 1)) + (mxu(high, low, dims(1, 1)) + mxu(low, high, dims(1, 1)))
    for ref, out in ((rows_ref, cols_ref), (cols_ref, rows_ref)):
        value = ref[...].T
        for k in range(len(slab_refs)):
            start = pl.multiple_of((me_ref[0] ^ k) * share, share)
            out[pl.ds(start, share), :] = value[k * share:(k + 1) * share, :]
    part_ref[...] = exact(rows_ref[...], omega_ref[...], dims(1, 1))


def mix_kernel(which, me_ref, factor_ref, *refs):
    count = factor_ref.shape[0] // refs[0].shape[0]
    slab_refs, out_refs, mixed = refs[:count], refs[-1 - len(which):-1], refs[-1]
    planes, share_k, share_z, width = out_refs[0].shape
    rows_y = slab_refs[0].shape[0]
    own = [factor_ref[pl.ds(pl.multiple_of((me_ref[0] ^ k) * rows_y, rows_y), rows_y), :] for k in range(count)]
    fac_high, fac_low = halves(jnp.concatenate(own, axis=0))
    high, low = halves(jnp.concatenate([ref[...] for ref in slab_refs], axis=0))
    mixed[...] = mxu(fac_high, high, dims(0, 0)) + (mxu(fac_high, low, dims(0, 0)) + mxu(fac_low, high, dims(0, 0)))
    for k, ref in zip(which, out_refs):
        start = pl.multiple_of((me_ref[0] ^ k) * share_k, share_k)
        block = mixed[pl.ds(start, share_k), :]
        for v in range(planes):
            at = lambda z: (v * share_z + z) * width
            rows = jnp.stack([block[:, at(z):at(z) + width] for z in range(share_z)], axis=0)
            ref[v] = jnp.swapaxes(rows, 0, 1)


def place_kernel(order, me_ref, *refs):
    *piece_refs, out_hbm, placed = refs
    share = piece_refs[0].shape[2]
    copies = []
    for k, ref in zip(order, piece_refs):
        start = pl.multiple_of((me_ref[0] ^ k) * share, share)
        copy = pltpu.make_async_copy(ref, out_hbm.at[:, :, pl.ds(start, share), :], placed.at[k])
        copy.start()
        copies.append(copy)
    for copy in copies:
        copy.wait()


def place(me, pieces, shape):
    order = steps(len(pieces)) + [0]
    return pl.pallas_call(
        functools.partial(place_kernel, order),
        in_specs=[SMEM] + [VMEM] * len(pieces),
        out_specs=pl.BlockSpec(memory_space=pltpu.HBM),
        out_shape=jax.ShapeDtypeStruct(shape, jnp.float32),
        scratch_shapes=[pltpu.SemaphoreType.DMA((len(pieces),))],
        compiler_params=pltpu.CompilerParams(vmem_limit_bytes=16 << 20),
        name="place",
    )(me, *[held(pieces[k]) for k in order])


def eliminate(gram, count, rank, out_ref):
    lanes = lax.broadcasted_iota(jnp.int32, (8, count), 1)
    subs = lax.broadcasted_iota(jnp.int32, (8, count), 0)
    blocks = count // 8
    full = lambda x: jnp.broadcast_to(x, (8, count))
    left = [gram[8 * b:8 * b + 8, :] for b in range(blocks)]
    right = [(lanes == subs + 8 * b).astype(jnp.float32) for b in range(blocks)]
    for j in range(0, count, 2):
        b, s = divmod(j, 8)
        l0, l1 = full(left[b][s:s + 1, :]), full(left[b][s + 1:s + 2, :])
        r0, r1 = full(right[b][s:s + 1, :]), full(right[b][s + 1:s + 2, :])
        p, q, t = full(l0[:, j:j + 1]), full(l0[:, j + 1:j + 2]), full(l1[:, j + 1:j + 2])
        inv = 1.0 / (p * t - q * q)
        ratio = q / p
        first = r0 * lax.rsqrt(p)
        second = (r1 - ratio * r0) * lax.rsqrt(t - q * ratio)
        out_ref[j:j + 1, :] = jnp.where(j < rank, first[0:1], 0.0)
        out_ref[j + 1:j + 2, :] = jnp.where(j + 1 < rank, second[0:1], 0.0)
        if j + 2 >= count:
            break
        u0 = (l0 * t - l1 * q) * inv
        u1 = (l1 * p - l0 * q) * inv
        v0 = (r0 * t - r1 * q) * inv
        v1 = (r1 * p - r0 * q) * inv
        for i in range(b, blocks):
            if i == b and s == 6:
                continue
            c0, c1 = full(left[i][:, j:j + 1]), full(left[i][:, j + 1:j + 2])
            if i == b:
                c0 = jnp.where(subs > s + 1, c0, 0.0)
                c1 = jnp.where(subs > s + 1, c1, 0.0)
            left[i] = left[i] - c0 * u0 - c1 * u1
            right[i] = right[i] - c0 * v0 - c1 * v1


def factor_x_kernel(scale, rank_ref, me_ref, *refs):
    *piece_refs, out_ref, sketch_ref = refs
    sketch_t = gather_sketch(scale, me_ref, piece_refs, sketch_ref)
    eliminate(exact(sketch_t, sketch_t, dims(1, 1)), sketch_t.shape[0], rank_ref[0], out_ref)


def inverse_factor_x(scale, rank, me, pieces):
    width = pieces[0].shape[0] * len(pieces)
    scratch = [pltpu.VMEM((width, pieces[0].shape[1]), jnp.float32)]
    kernel = functools.partial(factor_x_kernel, scale)
    return kernel_call(kernel, "factor_x", (width, width), [rank, me], pieces, scratch)


def apply_kernel(scale, me_ref, inverse_ref, *refs):
    *piece_refs, out_ref, whole = refs
    sketch_t = gather_sketch(scale, me_ref, piece_refs, whole)
    out_ref[...] = exact(sketch_t, inverse_ref[...], dims(0, 1))


def make_factor_x(scale, me, inverse, pieces):
    width, cells = inverse.shape[0], pieces[0].shape[1]
    scratch = [pltpu.VMEM((width, cells), jnp.float32)]
    kernel = functools.partial(apply_kernel, scale)
    return kernel_call(kernel, "apply", (cells, width), [me], [inverse] + pieces, scratch, whole_out=True)


def factor_y_kernel(divisor, rank_ref, *refs):
    *part_refs, out_ref, inverse = refs
    sketch = part_refs[0][...]
    for ref in part_refs[1:]:
        sketch = sketch + ref[...]
    sketch = sketch / divisor
    eliminate(exact(sketch, sketch, dims(0, 0)), sketch.shape[1], rank_ref[0], inverse)
    out_ref[...] = exact(sketch, inverse[...], dims(1, 1))


def make_factor_y(rank, parts, divisor):
    width = parts[0].shape[1]
    scratch = [pltpu.VMEM((width, width), jnp.float32)]
    kernel = functools.partial(factor_y_kernel, divisor)
    return kernel_call(kernel, "factor_y", parts[0].shape, [rank], parts, scratch)


def body(field, omega_x, omega_y, rank_x, rank_y):
    planes, rows_y, rows_z, cells_x = field.shape
    ranks_x = omega_x.shape[1]
    ranks_y = omega_y.shape[1]
    n_gy = lax.axis_size("gy")
    gy = lax.axis_index("gy")
    all_planes = planes * lax.axis_size("vert")
    all_rows_y = rows_y * n_gy
    all_rows_z = rows_z * lax.axis_size("gz")
    flat = field.reshape(-1, cells_x)

    here = gy[None].astype(jnp.int32)
    quarter = lax.axis_index("gz") * lax.axis_size("vert") + lax.axis_index("vert")
    n_quarter = lax.axis_size(("gz", "vert"))
    quarter = quarter[None].astype(jnp.int32)
    field_v, parts = sketch_parts(quarter, here, n_quarter, flat, omega_x)
    pieces = sum_sketch(parts)
    scale = 1.0 / float(all_planes * all_rows_y * all_rows_z)

    share_z = rows_z // n_gy
    share_k = ranks_y // n_gy
    field_z = field_v.reshape(planes * rows_y, rows_z, cells_x)
    tiled = share_z % 8 == 0 and share_k % 8 == 0
    if tiled:
        cut = lambda s, after: field_chunk(scale, s, [quarter, here], field_z, pieces, share_z, after)
    else:
        sketch_t = jnp.take(jnp.stack(pieces), quarter ^ jnp.arange(n_quarter), axis=0)
        sketch_t = sketch_t.reshape(ranks_x, cells_x) * scale
        raw = lax.dot_general(flat, sketch_t, dims(1, 1), precision=HIGH)
        raw = raw.reshape(planes * rows_y, rows_z, ranks_x)
        cut = lambda s, after: lax.dynamic_slice_in_dim(raw, (gy ^ s) * share_z, share_z, 1)
    chunks = [None] * n_gy
    after = pieces[0]
    for s in steps(n_gy):
        after = cut(s, after)
        chunks[s] = swap(after, "gy", s)
    chunks[0] = cut(0, after)

    inverse_x = inverse_factor_x(scale, rank_x, quarter, pieces)
    factor_x = make_factor_x(scale, quarter, inverse_x, pieces)

    if tiled:
        slabs = [None] * n_gy
        after = []
        for s in [0] + steps(n_gy):
            slabs[s] = lift(planes, inverse_x, chunks[s], after)
            after = [slabs[s]]
        scratch = [pltpu.VMEM((all_rows_y, all_rows_y), jnp.float32)] * 2
        shape = (all_rows_y, ranks_y)
        part_y = kernel_call(gram_kernel, "gram", shape, [here], [omega_y.T] + slabs, scratch)
    else:
        spread = jnp.stack(chunks).reshape(-1, ranks_x)
        spread = lax.dot_general(spread, inverse_x, dims(1, 1), precision=HIGH)
        spread = spread.reshape(n_gy, planes, rows_y, share_z, ranks_x)
        local_gram_y = jnp.einsum("gvazr,hvbzr->gahb", spread, spread, precision=HIGH)
        local_gram_y = local_gram_y.reshape(all_rows_y, all_rows_y)
        omega_p = by_step(omega_y.reshape(n_gy, rows_y, ranks_y), gy, n_gy).reshape(all_rows_y, ranks_y)
        part_y = jnp.dot(local_gram_y, omega_p, precision=HIGHEST)
        part_y = by_step(part_y.reshape(n_gy, rows_y, ranks_y), gy, n_gy).reshape(all_rows_y, ranks_y)
    for axis in ("vert", "gz"):
        count = lax.axis_size(axis)
        got = [swap(part_y, axis, s) for s in steps(count)]
        for other in got:
            part_y = part_y + other
    parts = [part_y] + [swap(part_y, "gy", s) for s in steps(n_gy)]
    factor_y = make_factor_y(rank_y, parts, float(all_planes * all_rows_z * ranks_x))

    if tiled:
        shape = (planes, share_k, share_z, ranks_x)
        scratch = [pltpu.VMEM((ranks_y, planes * share_z * ranks_x), jnp.float32)]

        which = steps(n_gy) + [0]
        kernel = functools.partial(mix_kernel, which)
        blocks = kernel_call(kernel, "mix", [shape] * n_gy, [here], [factor_y] + slabs, scratch)
        pieces = [None] * n_gy
        for s, block in zip(which, blocks):
            pieces[s] = swap(block, "gy", s) if s else block
        core = place(here, pieces, (planes, share_k, rows_z, ranks_x))
        return (core, factor_x, factor_y)
    weights = by_step(factor_y.reshape(n_gy, rows_y, ranks_y), gy, n_gy)
    weights = weights.reshape(n_gy, rows_y, n_gy, share_k)
    weights = jnp.moveaxis(by_step(jnp.moveaxis(weights, 2, 0), gy, n_gy), 0, 2)
    mixed = jnp.einsum("gvyzr,gyhk->hvkzr", spread, weights, precision=HIGH)
    pieces = [None] * n_gy
    for s in steps(n_gy):
        pieces[s] = swap(mixed[s], "gy", s)
    pieces[0] = mixed[0]
    core = by_step(jnp.stack(pieces), gy, n_gy)
    core = jnp.moveaxis(core, 0, 2).reshape(planes, share_k, rows_z, ranks_x)
    return (core, factor_x, factor_y)


def solution(mesh):
    in_specs = (P(("grp", "vert"), "gy", "gz", None), P(), P(), P("grp"), P("grp"))
    out_specs = (P(("grp", "vert"), "gy", "gz", None), P("grp", None), P("grp", None))
    return jax.shard_map(body, mesh=mesh, in_specs=in_specs, out_specs=out_specs, check_vma=False)
```

```python
import functools

import jax
import jax.numpy as jnp
from jax import lax
from jax.experimental import pallas as pl
from jax.experimental.pallas import tpu as pltpu
from jax.sharding import PartitionSpec as P

HIGH = lax.Precision.HIGH
HIGHEST = lax.Precision.HIGHEST


def swap(value, axes, step):
    count = lax.axis_size(axes)
    assert count & (count - 1) == 0
    return lax.ppermute(value, axes, [(i, i ^ step) for i in range(count)])


def steps(count):
    return sorted(range(1, count), key=lambda s: (s % 4 != 2, s))


def by_step(blocks, me, count):
    if count == 4:
        pairs = blocks.reshape((2, 2) + blocks.shape[1:])
        pairs = jnp.where(me & 2 != 0, pairs[::-1], pairs)
        pairs = jnp.where(me & 1 != 0, pairs[:, ::-1], pairs)
        return pairs.reshape(blocks.shape)
    return jnp.take(blocks, me ^ jnp.arange(count), axis=0)


def sum_over_gy(part):
    count = lax.axis_size("gy")
    got = [swap(part, "gy", s) for s in steps(count)]
    for other in got:
        part = part + other
    return part


def sum_sketch(parts):
    cores = lax.axis_size("vert")
    count = lax.axis_size("gz")
    sums = []
    for z in [*steps(count), 0]:
        total = parts[z * cores]
        for v in steps(cores):
            total = total + swap(parts[z * cores + v], "vert", v)
        sums.append(swap(total, "gz", z) if z else total)
    mine = sums[-1]
    for other in sums[:-1]:
        mine = mine + other
    mine = sum_over_gy(mine)
    pieces = [None] * (count * cores)
    for z in [*steps(count), 0]:
        pieces[z * cores] = swap(mine, "gz", z) if z else mine
        for v in steps(cores):
            pieces[z * cores + v] = swap(pieces[z * cores], "vert", v)
    return pieces


def dims(left, right):
    return (((left,), (right,)), ((), ()))


def mxu(a, b, numbers):
    return lax.dot_general(a, b, numbers, preferred_element_type=jnp.float32)


def exact(a, b, numbers):
    return lax.dot_general(a, b, numbers, precision=HIGHEST, preferred_element_type=jnp.float32)


def halves(value):
    high = value.astype(jnp.bfloat16)
    return high, (value - high.astype(jnp.float32)).astype(jnp.bfloat16)


VMEM = pl.BlockSpec(memory_space=pltpu.VMEM)
SMEM = pl.BlockSpec(memory_space=pltpu.SMEM)


def held(value):
    return pltpu.with_memory_space_constraint(value, pltpu.VMEM)


def kernel_call(body, name, out_shape, scalars, values, scratch=(), limit=16, whole_out=False):
    many = isinstance(out_shape, list)
    shapes = out_shape if many else [out_shape]
    if whole_out:
        outs = [jax.ShapeDtypeStruct(shape, jnp.float32) for shape in shapes]
    else:
        outs = [pltpu.VMEM(shape, jnp.float32) for shape in shapes]
    return pl.pallas_call(
        body,
        in_specs=[SMEM] * len(scalars) + [VMEM] * len(values),
        out_specs=[VMEM] * len(outs) if many else VMEM,
        out_shape=outs if many else outs[0],
        scratch_shapes=list(scratch),
        compiler_params=pltpu.CompilerParams(vmem_limit_bytes=limit << 20),
        name=name,
    )(*scalars, *[held(value) for value in values])


PIECES = 3


def sketch_kernel(me_ref, here_ref, field_hbm, omega_hbm, field_ref, *refs):
    *part_refs, omega_ref, total, arrived = refs
    omega_copy = pltpu.make_async_copy(omega_hbm, omega_ref, arrived.at[PIECES])
    omega_copy.start()
    width = omega_ref.shape[1]
    eighth = field_ref.shape[0] // 8
    ends = [0, 2 * eighth, 5 * eighth, 8 * eighth]
    copies = []
    for i in range(PIECES):
        rows = pl.ds(ends[i], ends[i + 1] - ends[i])
        copies.append(pltpu.make_async_copy(field_hbm.at[rows], field_ref.at[rows], arrived.at[i]))
        copies[i].start()
    omega_copy.wait()
    omega_high, omega_low = halves(omega_ref[...])
    omega_both = jnp.concatenate([omega_high, omega_low], axis=1)
    wide = narrow = None
    for i in range(PIECES):
        copies[i].wait()
        high, low = halves(field_ref[ends[i]:ends[i + 1], :])
        both = mxu(high, omega_both, dims(1, 0))
        projected = both[:, :width] + (both[:, width:] + mxu(low, omega_high, dims(1, 0)))
        proj_high, proj_low = halves(projected)
        first = mxu(jnp.concatenate([proj_high, proj_low], axis=1), high, dims(0, 0))
        second = mxu(proj_high, low, dims(0, 0))
        wide = first if wide is None else wide + first
        narrow = second if narrow is None else narrow + second
    total[...] = wide[:width, :] + (wide[width:, :] + narrow)
    share = width // len(part_refs)
    for k, ref in enumerate(part_refs):
        start = pl.multiple_of((me_ref[0] ^ k) * share, share)
        ref[...] = total[pl.ds(start, share), :]


def sketch_parts(me, here, count, flat, omega):
    rows, cells = flat.shape
    width = omega.shape[1]
    far = pl.BlockSpec(memory_space=pltpu.HBM)
    out = pl.pallas_call(
        sketch_kernel,
        in_specs=[SMEM, SMEM, far, far],
        out_specs=[VMEM] * (1 + count),
        out_shape=[pltpu.VMEM((rows, cells), jnp.float32)]
        + [pltpu.VMEM((width // count, cells), jnp.float32)] * count,
        scratch_shapes=[
            pltpu.VMEM((cells, width), jnp.float32),
            pltpu.VMEM((width, cells), jnp.float32),
            pltpu.SemaphoreType.DMA((PIECES + 1,)),
        ],
        compiler_params=pltpu.CompilerParams(vmem_limit_bytes=24 << 20),
        name="sketch",
    )(me, here, *[pltpu.with_memory_space_constraint(x, pltpu.HBM) for x in (flat, omega)])
    return out[0], out[1:]


def gather_sketch(scale, me_ref, piece_refs, whole):
    share = piece_refs[0].shape[0]
    for k, ref in enumerate(piece_refs):
        start = pl.multiple_of((me_ref[0] ^ k) * share, share)
        whole[pl.ds(start, share), :] = ref[...] * scale
    return whole[...]


def chunk_kernel(scale, step, me_ref, here_ref, field_ref, *refs):
    *piece_refs, _, out_ref, whole = refs
    sketch = gather_sketch(scale, me_ref, piece_refs, whole)
    width, cells = sketch.shape
    rows, share, _ = out_ref.shape
    start = pl.multiple_of((here_ref[0] ^ step) * share, share)
    high, low = halves(field_ref[:, pl.ds(start, share), :].reshape(rows * share, cells))
    sketch_high, sketch_low = halves(sketch)
    both = mxu(high, jnp.concatenate([sketch_high, sketch_low], axis=0), dims(1, 1))
    raw = both[:, :width] + (both[:, width:] + mxu(low, sketch_high, dims(1, 1)))
    out_ref[...] = raw.reshape(rows, share, width)


def field_chunk(scale, step, places, field, pieces, share, after):
    width, cells = pieces[0].shape[0] * len(pieces), field.shape[2]
    scratch = [pltpu.VMEM((width, cells), jnp.float32)]
    kernel = functools.partial(chunk_kernel, scale, step)
    shape = (field.shape[0], share, width)
    return kernel_call(kernel, "chunk", shape, places, [field] + pieces + [after], scratch)


def lift_kernel(planes, inverse_ref, chunk_ref, *refs):
    out_ref = refs[-1]
    rows, share, width = chunk_ref.shape
    inv_high, inv_low = halves(inverse_ref[...])
    high, low = halves(chunk_ref[...].reshape(rows * share, width))
    both = mxu(high, jnp.concatenate([inv_high, inv_low], axis=0), dims(1, 1))
    value = both[:, :width] + (both[:, width:] + mxu(low, inv_high, dims(1, 1)))
    value = jnp.swapaxes(value.reshape(planes, rows // planes, share, width), 1, 2)
    for v in range(planes):
        for z in range(share):
            at = (v * share + z) * width
            out_ref[:, at:at + width] = value[v, z]


def lift(planes, inverse, chunk, after):
    rows, share, width = chunk.shape
    shape = (rows // planes, planes * share * width)
    return kernel_call(functools.partial(lift_kernel, planes), "lift", shape, [], [inverse, chunk] + after)


def gram_kernel(me_ref, omega_ref, *refs):
    *slab_refs, part_ref, rows_ref, cols_ref = refs
    share = slab_refs[0].shape[0]
    high, low = halves(jnp.concatenate([ref[...] for ref in slab_refs], axis=0))
    rows_ref[...] = mxu(high, high, dims(1, 1)) + (mxu(high, low, dims(1, 1)) + mxu(low, high, dims(1, 1)))
    for ref, out in ((rows_ref, cols_ref), (cols_ref, rows_ref)):
        value = ref[...].T
        for k in range(len(slab_refs)):
            start = pl.multiple_of((me_ref[0] ^ k) * share, share)
            out[pl.ds(start, share), :] = value[k * share:(k + 1) * share, :]
    part_ref[...] = exact(rows_ref[...], omega_ref[...], dims(1, 1))


def mix_kernel(which, me_ref, factor_ref, *refs):
    count = factor_ref.shape[0] // refs[0].shape[0]
    slab_refs, out_refs, mixed = refs[:count], refs[-1 - len(which):-1], refs[-1]
    planes, share_k, share_z, width = out_refs[0].shape
    rows_y = slab_refs[0].shape[0]
    own = [factor_ref[pl.ds(pl.multiple_of((me_ref[0] ^ k) * rows_y, rows_y), rows_y), :] for k in range(count)]
    fac_high, fac_low = halves(jnp.concatenate(own, axis=0))
    high, low = halves(jnp.concatenate([ref[...] for ref in slab_refs], axis=0))
    mixed[...] = mxu(fac_high, high, dims(0, 0)) + (mxu(fac_high, low, dims(0, 0)) + mxu(fac_low, high, dims(0, 0)))
    for k, ref in zip(which, out_refs):
        start = pl.multiple_of((me_ref[0] ^ k) * share_k, share_k)
        block = mixed[pl.ds(start, share_k), :]
        for v in range(planes):
            at = lambda z: (v * share_z + z) * width
            rows = jnp.stack([block[:, at(z):at(z) + width] for z in range(share_z)], axis=0)
            ref[v] = jnp.swapaxes(rows, 0, 1)


def place_kernel(order, me_ref, *refs):
    *piece_refs, out_hbm, placed = refs
    share = piece_refs[0].shape[2]
    copies = []
    for k, ref in zip(order, piece_refs):
        start = pl.multiple_of((me_ref[0] ^ k) * share, share)
        copy = pltpu.make_async_copy(ref, out_hbm.at[:, :, pl.ds(start, share), :], placed.at[k])
        copy.start()
        copies.append(copy)
    for copy in copies:
        copy.wait()


def place(me, pieces, shape):
    order = steps(len(pieces)) + [0]
    return pl.pallas_call(
        functools.partial(place_kernel, order),
        in_specs=[SMEM] + [VMEM] * len(pieces),
        out_specs=pl.BlockSpec(memory_space=pltpu.HBM),
        out_shape=jax.ShapeDtypeStruct(shape, jnp.float32),
        scratch_shapes=[pltpu.SemaphoreType.DMA((len(pieces),))],
        compiler_params=pltpu.CompilerParams(vmem_limit_bytes=16 << 20),
        name="place",
    )(me, *[held(pieces[k]) for k in order])


def eliminate(gram, count, rank, out_ref):
    lanes = lax.broadcasted_iota(jnp.int32, (8, count), 1)
    subs = lax.broadcasted_iota(jnp.int32, (8, count), 0)
    blocks = count // 8
    full = lambda x: jnp.broadcast_to(x, (8, count))
    left = [gram[8 * b:8 * b + 8, :] for b in range(blocks)]
    right = [(lanes == subs + 8 * b).astype(jnp.float32) for b in range(blocks)]
    for b in range(blocks):
        at = 8 * b
        l = [full(left[b][k:k + 1, :]) for k in range(8)]
        r = [full(right[b][k:k + 1, :]) for k in range(8)]
        a = {(k, m): full(l[k][:, at + m:at + m + 1]) for k in range(8) for m in range(k, 8)}
        inv, f = {}, {}
        for k in range(8):
            inv[k] = 1.0 / a[k, k]
            for m in range(k + 1, 8):
                f[k, m] = a[k, m] * inv[k]
                for q in range(m, 8):
                    a[m, q] = a[m, q] - f[k, m] * a[k, q]
                l[m] = l[m] - f[k, m] * l[k]
                r[m] = r[m] - f[k, m] * r[k]
            row = (r[k] * lax.rsqrt(a[k, k]))[0:1]
            out_ref[at + k:at + k + 1, :] = jnp.where(at + k < rank, row, 0.0)
        if b + 1 == blocks:
            break
        w, v = {}, {}
        for k in reversed(range(8)):
            w[k], v[k] = l[k] * inv[k], r[k] * inv[k]
            for m in range(k + 1, 8):
                w[k] = w[k] - f[k, m] * w[m]
                v[k] = v[k] - f[k, m] * v[m]
        for i in range(b + 1, blocks):
            column = [full(left[i][:, at + k:at + k + 1]) for k in range(8)]
            for k in range(8):
                left[i] = left[i] - column[k] * w[k]
                right[i] = right[i] - column[k] * v[k]


def factor_x_kernel(scale, rank_ref, me_ref, *refs):
    *piece_refs, out_ref, sketch_ref = refs
    sketch_t = gather_sketch(scale, me_ref, piece_refs, sketch_ref)
    eliminate(exact(sketch_t, sketch_t, dims(1, 1)), sketch_t.shape[0], rank_ref[0], out_ref)


def inverse_factor_x(scale, rank, me, pieces):
    width = pieces[0].shape[0] * len(pieces)
    scratch = [pltpu.VMEM((width, pieces[0].shape[1]), jnp.float32)]
    kernel = functools.partial(factor_x_kernel, scale)
    return kernel_call(kernel, "factor_x", (width, width), [rank, me], pieces, scratch)


def apply_kernel(scale, me_ref, inverse_ref, *refs):
    *piece_refs, out_ref, whole = refs
    sketch_t = gather_sketch(scale, me_ref, piece_refs, whole)
    out_ref[...] = exact(sketch_t, inverse_ref[...], dims(0, 1))


def make_factor_x(scale, me, inverse, pieces):
    width, cells = inverse.shape[0], pieces[0].shape[1]
    scratch = [pltpu.VMEM((width, cells), jnp.float32)]
    kernel = functools.partial(apply_kernel, scale)
    return kernel_call(kernel, "apply", (cells, width), [me], [inverse] + pieces, scratch, whole_out=True)


def factor_y_kernel(divisor, rank_ref, *refs):
    *part_refs, out_ref, inverse = refs
    sketch = part_refs[0][...]
    for ref in part_refs[1:]:
        sketch = sketch + ref[...]
    sketch = sketch / divisor
    eliminate(exact(sketch, sketch, dims(0, 0)), sketch.shape[1], rank_ref[0], inverse)
    out_ref[...] = exact(sketch, inverse[...], dims(1, 1))


def make_factor_y(rank, parts, divisor):
    width = parts[0].shape[1]
    scratch = [pltpu.VMEM((width, width), jnp.float32)]
    kernel = functools.partial(factor_y_kernel, divisor)
    return kernel_call(kernel, "factor_y", parts[0].shape, [rank], parts, scratch)


def body(field, omega_x, omega_y, rank_x, rank_y):
    planes, rows_y, rows_z, cells_x = field.shape
    ranks_x = omega_x.shape[1]
    ranks_y = omega_y.shape[1]
    n_gy = lax.axis_size("gy")
    gy = lax.axis_index("gy")
    all_planes = planes * lax.axis_size("vert")
    all_rows_y = rows_y * n_gy
    all_rows_z = rows_z * lax.axis_size("gz")
    flat = field.reshape(-1, cells_x)

    here = gy[None].astype(jnp.int32)
    quarter = lax.axis_index("gz") * lax.axis_size("vert") + lax.axis_index("vert")
    n_quarter = lax.axis_size(("gz", "vert"))
    quarter = quarter[None].astype(jnp.int32)
    field_v, parts = sketch_parts(quarter, here, n_quarter, flat, omega_x)
    pieces = sum_sketch(parts)
    scale = 1.0 / float(all_planes * all_rows_y * all_rows_z)

    share_z = rows_z // n_gy
    share_k = ranks_y // n_gy
    field_z = field_v.reshape(planes * rows_y, rows_z, cells_x)
    tiled = share_z % 8 == 0 and share_k % 8 == 0
    if tiled:
        cut = lambda s, after: field_chunk(scale, s, [quarter, here], field_z, pieces, share_z, after)
    else:
        sketch_t = jnp.take(jnp.stack(pieces), quarter ^ jnp.arange(n_quarter), axis=0)
        sketch_t = sketch_t.reshape(ranks_x, cells_x) * scale
        raw = lax.dot_general(flat, sketch_t, dims(1, 1), precision=HIGH)
        raw = raw.reshape(planes * rows_y, rows_z, ranks_x)
        cut = lambda s, after: lax.dynamic_slice_in_dim(raw, (gy ^ s) * share_z, share_z, 1)
    chunks = [None] * n_gy
    after = pieces[0]
    for s in steps(n_gy):
        after = cut(s, after)
        chunks[s] = swap(after, "gy", s)
    chunks[0] = cut(0, after)

    inverse_x = inverse_factor_x(scale, rank_x, quarter, pieces)
    factor_x = make_factor_x(scale, quarter, inverse_x, pieces)

    if tiled:
        slabs = [None] * n_gy
        after = []
        for s in [0] + steps(n_gy):
            slabs[s] = lift(planes, inverse_x, chunks[s], after)
            after = [slabs[s]]
        scratch = [pltpu.VMEM((all_rows_y, all_rows_y), jnp.float32)] * 2
        shape = (all_rows_y, ranks_y)
        part_y = kernel_call(gram_kernel, "gram", shape, [here], [omega_y.T] + slabs, scratch)
    else:
        spread = jnp.stack(chunks).reshape(-1, ranks_x)
        spread = lax.dot_general(spread, inverse_x, dims(1, 1), precision=HIGH)
        spread = spread.reshape(n_gy, planes, rows_y, share_z, ranks_x)
        local_gram_y = jnp.einsum("gvazr,hvbzr->gahb", spread, spread, precision=HIGH)
        local_gram_y = local_gram_y.reshape(all_rows_y, all_rows_y)
        omega_p = by_step(omega_y.reshape(n_gy, rows_y, ranks_y), gy, n_gy).reshape(all_rows_y, ranks_y)
        part_y = jnp.dot(local_gram_y, omega_p, precision=HIGHEST)
        part_y = by_step(part_y.reshape(n_gy, rows_y, ranks_y), gy, n_gy).reshape(all_rows_y, ranks_y)
    for axis in ("vert", "gz"):
        count = lax.axis_size(axis)
        got = [swap(part_y, axis, s) for s in steps(count)]
        for other in got:
            part_y = part_y + other
    parts = [part_y] + [swap(part_y, "gy", s) for s in steps(n_gy)]
    factor_y = make_factor_y(rank_y, parts, float(all_planes * all_rows_z * ranks_x))

    if tiled:
        shape = (planes, share_k, share_z, ranks_x)
        scratch = [pltpu.VMEM((ranks_y, planes * share_z * ranks_x), jnp.float32)]

        which = steps(n_gy) + [0]
        kernel = functools.partial(mix_kernel, which)
        blocks = kernel_call(kernel, "mix", [shape] * n_gy, [here], [factor_y] + slabs, scratch)
        pieces = [None] * n_gy
        for s, block in zip(which, blocks):
            pieces[s] = swap(block, "gy", s) if s else block
        core = place(here, pieces, (planes, share_k, rows_z, ranks_x))
        return (core, factor_x, factor_y)
    weights = by_step(factor_y.reshape(n_gy, rows_y, ranks_y), gy, n_gy)
    weights = weights.reshape(n_gy, rows_y, n_gy, share_k)
    weights = jnp.moveaxis(by_step(jnp.moveaxis(weights, 2, 0), gy, n_gy), 0, 2)
    mixed = jnp.einsum("gvyzr,gyhk->hvkzr", spread, weights, precision=HIGH)
    pieces = [None] * n_gy
    for s in steps(n_gy):
        pieces[s] = swap(mixed[s], "gy", s)
    pieces[0] = mixed[0]
    core = by_step(jnp.stack(pieces), gy, n_gy)
    core = jnp.moveaxis(core, 0, 2).reshape(planes, share_k, rows_z, ranks_x)
    return (core, factor_x, factor_y)


def solution(mesh):
    in_specs = (P(("grp", "vert"), "gy", "gz", None), P(), P(), P("grp"), P("grp"))
    out_specs = (P(("grp", "vert"), "gy", "gz", None), P("grp", None), P("grp", None))
    return jax.shard_map(body, mesh=mesh, in_specs=in_specs, out_specs=out_specs, check_vma=False)
```

```python
import functools

import jax
import jax.numpy as jnp
from jax import lax
from jax.experimental import pallas as pl
from jax.experimental.pallas import tpu as pltpu
from jax.sharding import PartitionSpec as P

HIGH = lax.Precision.HIGH
HIGHEST = lax.Precision.HIGHEST


def swap(value, axes, step):
    count = lax.axis_size(axes)
    assert count & (count - 1) == 0
    return lax.ppermute(value, axes, [(i, i ^ step) for i in range(count)])


def steps(count):
    return sorted(range(1, count), key=lambda s: (s % 4 != 2, s))


def by_step(blocks, me, count):
    if count == 4:
        pairs = blocks.reshape((2, 2) + blocks.shape[1:])
        pairs = jnp.where(me & 2 != 0, pairs[::-1], pairs)
        pairs = jnp.where(me & 1 != 0, pairs[:, ::-1], pairs)
        return pairs.reshape(blocks.shape)
    return jnp.take(blocks, me ^ jnp.arange(count), axis=0)


def sum_over_gy(part):
    count = lax.axis_size("gy")
    got = [swap(part, "gy", s) for s in steps(count)]
    for other in got:
        part = part + other
    return part


def sum_sketch(parts):
    cores = lax.axis_size("vert")
    count = lax.axis_size("gz")
    sums = []
    for z in [*steps(count), 0]:
        total = parts[z * cores]
        for v in steps(cores):
            total = total + swap(parts[z * cores + v], "vert", v)
        sums.append(swap(total, "gz", z) if z else total)
    mine = sums[-1]
    for other in sums[:-1]:
        mine = mine + other
    mine = sum_over_gy(mine)
    return [mine] + [swap(mine, ("gz", "vert"), k) for k in range(1, count * cores)]


def dims(left, right):
    return (((left,), (right,)), ((), ()))


def mxu(a, b, numbers):
    return lax.dot_general(a, b, numbers, preferred_element_type=jnp.float32)


def exact(a, b, numbers):
    return lax.dot_general(a, b, numbers, precision=HIGHEST, preferred_element_type=jnp.float32)


def halves(value):
    high = value.astype(jnp.bfloat16)
    return high, (value - high.astype(jnp.float32)).astype(jnp.bfloat16)


VMEM = pl.BlockSpec(memory_space=pltpu.VMEM)
SMEM = pl.BlockSpec(memory_space=pltpu.SMEM)


def held(value):
    return pltpu.with_memory_space_constraint(value, pltpu.VMEM)


def kernel_call(body, name, out_shape, scalars, values, scratch=(), limit=16, whole_out=False):
    many = isinstance(out_shape, list)
    shapes = out_shape if many else [out_shape]
    if whole_out:
        outs = [jax.ShapeDtypeStruct(shape, jnp.float32) for shape in shapes]
    else:
        outs = [pltpu.VMEM(shape, jnp.float32) for shape in shapes]
    return pl.pallas_call(
        body,
        in_specs=[SMEM] * len(scalars) + [VMEM] * len(values),
        out_specs=[VMEM] * len(outs) if many else VMEM,
        out_shape=outs if many else outs[0],
        scratch_shapes=list(scratch),
        compiler_params=pltpu.CompilerParams(vmem_limit_bytes=limit << 20),
        name=name,
    )(*scalars, *[held(value) for value in values])


PIECES = 3


def sketch_kernel(me_ref, here_ref, field_hbm, omega_hbm, field_ref, *refs):
    *part_refs, omega_ref, total, arrived = refs
    omega_copy = pltpu.make_async_copy(omega_hbm, omega_ref, arrived.at[PIECES])
    omega_copy.start()
    width = omega_ref.shape[1]
    eighth = field_ref.shape[0] // 8
    ends = [0, 2 * eighth, 5 * eighth, 8 * eighth]
    copies = []
    for i in range(PIECES):
        rows = pl.ds(ends[i], ends[i + 1] - ends[i])
        copies.append(pltpu.make_async_copy(field_hbm.at[rows], field_ref.at[rows], arrived.at[i]))
        copies[i].start()
    omega_copy.wait()
    omega_high, omega_low = halves(omega_ref[...])
    omega_both = jnp.concatenate([omega_high, omega_low], axis=1)
    wide = narrow = None
    for i in range(PIECES):
        copies[i].wait()
        high, low = halves(field_ref[ends[i]:ends[i + 1], :])
        both = mxu(high, omega_both, dims(1, 0))
        projected = both[:, :width] + (both[:, width:] + mxu(low, omega_high, dims(1, 0)))
        proj_high, proj_low = halves(projected)
        first = mxu(jnp.concatenate([proj_high, proj_low], axis=1), high, dims(0, 0))
        second = mxu(proj_high, low, dims(0, 0))
        wide = first if wide is None else wide + first
        narrow = second if narrow is None else narrow + second
    total[...] = wide[:width, :] + (wide[width:, :] + narrow)
    share = width // len(part_refs)
    for k, ref in enumerate(part_refs):
        start = pl.multiple_of((me_ref[0] ^ k) * share, share)
        ref[...] = total[pl.ds(start, share), :]


def sketch_parts(me, here, count, flat, omega):
    rows, cells = flat.shape
    width = omega.shape[1]
    far = pl.BlockSpec(memory_space=pltpu.HBM)
    out = pl.pallas_call(
        sketch_kernel,
        in_specs=[SMEM, SMEM, far, far],
        out_specs=[VMEM] * (1 + count),
        out_shape=[pltpu.VMEM((rows, cells), jnp.float32)]
        + [pltpu.VMEM((width // count, cells), jnp.float32)] * count,
        scratch_shapes=[
            pltpu.VMEM((cells, width), jnp.float32),
            pltpu.VMEM((width, cells), jnp.float32),
            pltpu.SemaphoreType.DMA((PIECES + 1,)),
        ],
        compiler_params=pltpu.CompilerParams(vmem_limit_bytes=24 << 20),
        name="sketch",
    )(me, here, *[pltpu.with_memory_space_constraint(x, pltpu.HBM) for x in (flat, omega)])
    return out[0], out[1:]


def gather_sketch(scale, me_ref, piece_refs, whole):
    share = piece_refs[0].shape[0]
    for k, ref in enumerate(piece_refs):
        start = pl.multiple_of((me_ref[0] ^ k) * share, share)
        whole[pl.ds(start, share), :] = ref[...] * scale
    return whole[...]


def chunk_kernel(scale, step, many, here_ref, field_ref, *refs):
    piece_refs, out_ref = refs[:many], refs[-1]
    sketch = jnp.concatenate([ref[...] for ref in piece_refs], axis=0) * scale
    count = sketch.shape[0]
    rows, _, cells = field_ref.shape
    share = out_ref.shape[1] // rows
    start = pl.multiple_of((here_ref[0] ^ step) * share, share)
    high, low = halves(field_ref[:, pl.ds(start, share), :].reshape(rows * share, cells))
    sketch_high, sketch_low = halves(sketch)
    both = mxu(jnp.concatenate([sketch_high, sketch_low], axis=0), high, dims(1, 1))
    out_ref[...] = both[:count] + (both[count:] + mxu(sketch_high, low, dims(1, 1)))


def field_chunk(scale, step, here, field, pieces, share, after):
    kernel = functools.partial(chunk_kernel, scale, step, len(pieces))
    shape = (sum(piece.shape[0] for piece in pieces), field.shape[0] * share)
    return kernel_call(kernel, "chunk", shape, [here], [field] + pieces + after)


def lift_kernel(planes, share, count, inverse_ref, *refs):
    out_ref = refs[-1]
    inv_high, inv_low = halves(inverse_ref[...])
    width = inv_high.shape[1]
    high, low = halves(jnp.concatenate([ref[...] for ref in refs[:count]], axis=0))
    both = mxu(high, jnp.concatenate([inv_high, inv_low], axis=1), dims(0, 0))
    value = both[:, :width] + (both[:, width:] + mxu(low, inv_high, dims(0, 0)))
    value = jnp.swapaxes(value.reshape(planes, out_ref.shape[0], share, width), 1, 2)
    for v in range(planes):
        for z in range(share):
            at = (v * share + z) * width
            out_ref[:, at:at + width] = value[v, z]


def lift(planes, share, inverse, chunk, after):
    samples, width = chunk[0].shape[1], inverse.shape[1]
    shape = (samples // (planes * share), planes * share * width)
    kernel = functools.partial(lift_kernel, planes, share, len(chunk))
    return kernel_call(kernel, "lift", shape, [], [inverse] + chunk + after)


def gram_kernel(me_ref, omega_ref, *refs):
    *slab_refs, part_ref, rows_ref, cols_ref = refs
    share = slab_refs[0].shape[0]
    high, low = halves(jnp.concatenate([ref[...] for ref in slab_refs], axis=0))
    rows_ref[...] = mxu(high, high, dims(1, 1)) + (mxu(high, low, dims(1, 1)) + mxu(low, high, dims(1, 1)))
    for ref, out in ((rows_ref, cols_ref), (cols_ref, rows_ref)):
        value = ref[...].T
        for k in range(len(slab_refs)):
            start = pl.multiple_of((me_ref[0] ^ k) * share, share)
            out[pl.ds(start, share), :] = value[k * share:(k + 1) * share, :]
    part_ref[...] = exact(rows_ref[...], omega_ref[...], dims(1, 1))


def mix_kernel(which, me_ref, factor_ref, *refs):
    count = factor_ref.shape[0] // refs[0].shape[0]
    slab_refs, out_refs, mixed = refs[:count], refs[-1 - len(which):-1], refs[-1]
    planes, share_k, share_z, width = out_refs[0].shape
    rows_y = slab_refs[0].shape[0]
    own = [factor_ref[pl.ds(pl.multiple_of((me_ref[0] ^ k) * rows_y, rows_y), rows_y), :] for k in range(count)]
    fac_high, fac_low = halves(jnp.concatenate(own, axis=0))
    high, low = halves(jnp.concatenate([ref[...] for ref in slab_refs], axis=0))
    mixed[...] = mxu(fac_high, high, dims(0, 0)) + (mxu(fac_high, low, dims(0, 0)) + mxu(fac_low, high, dims(0, 0)))
    for k, ref in zip(which, out_refs):
        start = pl.multiple_of((me_ref[0] ^ k) * share_k, share_k)
        block = mixed[pl.ds(start, share_k), :]
        for v in range(planes):
            at = lambda z: (v * share_z + z) * width
            rows = jnp.stack([block[:, at(z):at(z) + width] for z in range(share_z)], axis=0)
            ref[v] = jnp.swapaxes(rows, 0, 1)


def place_kernel(order, me_ref, *refs):
    *piece_refs, out_hbm, placed = refs
    share = piece_refs[0].shape[2]
    copies = []
    for k, ref in zip(order, piece_refs):
        start = pl.multiple_of((me_ref[0] ^ k) * share, share)
        copy = pltpu.make_async_copy(ref, out_hbm.at[:, :, pl.ds(start, share), :], placed.at[k])
        copy.start()
        copies.append(copy)
    for copy in copies:
        copy.wait()


def place(me, pieces, shape):
    order = steps(len(pieces)) + [0]
    return pl.pallas_call(
        functools.partial(place_kernel, order),
        in_specs=[SMEM] + [VMEM] * len(pieces),
        out_specs=pl.BlockSpec(memory_space=pltpu.HBM),
        out_shape=jax.ShapeDtypeStruct(shape, jnp.float32),
        scratch_shapes=[pltpu.SemaphoreType.DMA((len(pieces),))],
        compiler_params=pltpu.CompilerParams(vmem_limit_bytes=16 << 20),
        name="place",
    )(me, *[held(pieces[k]) for k in order])


def eliminate(gram, count, rank, out_ref):
    lanes = lax.broadcasted_iota(jnp.int32, (8, count), 1)
    subs = lax.broadcasted_iota(jnp.int32, (8, count), 0)
    blocks = count // 8
    full = lambda x: jnp.broadcast_to(x, (8, count))
    left = [gram[8 * b:8 * b + 8, :] for b in range(blocks)]
    right = [(lanes == subs + 8 * b).astype(jnp.float32) for b in range(blocks)]
    for b in range(blocks):
        at = 8 * b
        l = [full(left[b][k:k + 1, :]) for k in range(8)]
        r = [full(right[b][k:k + 1, :]) for k in range(8)]
        a = {(k, m): full(l[k][:, at + m:at + m + 1]) for k in range(8) for m in range(k, 8)}
        inv, f = {}, {}
        for k in range(8):
            inv[k] = 1.0 / a[k, k]
            for m in range(k + 1, 8):
                f[k, m] = a[k, m] * inv[k]
                for q in range(m, 8):
                    a[m, q] = a[m, q] - f[k, m] * a[k, q]
                l[m] = l[m] - f[k, m] * l[k]
                r[m] = r[m] - f[k, m] * r[k]
            row = (r[k] * lax.rsqrt(a[k, k]))[0:1]
            out_ref[at + k:at + k + 1, :] = jnp.where(at + k < rank, row, 0.0)
        if b + 1 == blocks:
            break
        w, v = {}, {}
        for k in reversed(range(8)):
            w[k], v[k] = l[k] * inv[k], r[k] * inv[k]
            for m in range(k + 1, 8):
                w[k] = w[k] - f[k, m] * w[m]
                v[k] = v[k] - f[k, m] * v[m]
        for i in range(b + 1, blocks):
            column = [full(left[i][:, at + k:at + k + 1]) for k in range(8)]
            for k in range(8):
                left[i] = left[i] - column[k] * w[k]
                right[i] = right[i] - column[k] * v[k]


def factor_x_kernel(scale, rank_ref, me_ref, *refs):
    *piece_refs, out_ref, sketch_ref, inverse_ref = refs
    sketch_t = gather_sketch(scale, me_ref, piece_refs, sketch_ref)
    eliminate(exact(sketch_t, sketch_t, dims(1, 1)), sketch_t.shape[0], rank_ref[0], inverse_ref)
    inverse_ref[...] = inverse_ref[...].T
    share = piece_refs[0].shape[0]
    for k in range(len(piece_refs)):
        start = pl.multiple_of((me_ref[0] ^ k) * share, share)
        out_ref[k * share:(k + 1) * share, :] = inverse_ref[pl.ds(start, share), :]


def inverse_factor_x(scale, rank, me, pieces):
    width = pieces[0].shape[0] * len(pieces)
    scratch = [pltpu.VMEM((width, pieces[0].shape[1]), jnp.float32), pltpu.VMEM((width, width), jnp.float32)]
    kernel = functools.partial(factor_x_kernel, scale)
    return kernel_call(kernel, "factor_x", (width, width), [rank, me], pieces, scratch)


def apply_kernel(scale, inverse_ref, *refs):
    *piece_refs, out_ref = refs
    sketch = jnp.concatenate([ref[...] for ref in piece_refs], axis=0) * scale
    out_ref[...] = exact(sketch, inverse_ref[...], dims(0, 0))


def make_factor_x(scale, inverse, pieces):
    shape = (pieces[0].shape[1], inverse.shape[1])
    kernel = functools.partial(apply_kernel, scale)
    return kernel_call(kernel, "apply", shape, [], [inverse] + pieces, whole_out=True)


def factor_y_kernel(divisor, rank_ref, *refs):
    *part_refs, out_ref, inverse = refs
    sketch = part_refs[0][...]
    for ref in part_refs[1:]:
        sketch = sketch + ref[...]
    sketch = sketch / divisor
    eliminate(exact(sketch, sketch, dims(0, 0)), sketch.shape[1], rank_ref[0], inverse)
    out_ref[...] = exact(sketch, inverse[...], dims(1, 1))


def make_factor_y(rank, parts, divisor):
    width = parts[0].shape[1]
    scratch = [pltpu.VMEM((width, width), jnp.float32)]
    kernel = functools.partial(factor_y_kernel, divisor)
    return kernel_call(kernel, "factor_y", parts[0].shape, [rank], parts, scratch)


def body(field, omega_x, omega_y, rank_x, rank_y):
    planes, rows_y, rows_z, cells_x = field.shape
    ranks_x = omega_x.shape[1]
    ranks_y = omega_y.shape[1]
    n_gy = lax.axis_size("gy")
    gy = lax.axis_index("gy")
    all_planes = planes * lax.axis_size("vert")
    all_rows_y = rows_y * n_gy
    all_rows_z = rows_z * lax.axis_size("gz")
    flat = field.reshape(-1, cells_x)

    here = gy[None].astype(jnp.int32)
    quarter = lax.axis_index("gz") * lax.axis_size("vert") + lax.axis_index("vert")
    n_quarter = lax.axis_size(("gz", "vert"))
    quarter = quarter[None].astype(jnp.int32)
    field_v, parts = sketch_parts(quarter, here, n_quarter, flat, omega_x)
    pieces = sum_sketch(parts)
    scale = 1.0 / float(all_planes * all_rows_y * all_rows_z)

    share_z = rows_z // n_gy
    share_k = ranks_y // n_gy
    field_z = field_v.reshape(planes * rows_y, rows_z, cells_x)
    tiled = share_z % 8 == 0 and share_k % 8 == 0
    order = steps(n_gy)
    chunks = [[] for _ in range(n_gy)]
    if tiled:
        after, ahead = [], []
        for s in order:
            if s & 2:
                part = field_chunk(scale, s, here, field_z, pieces[:1], share_z, after)
                after = [part]
                chunks[s].append(swap(part, "gy", s))
                ahead.append(chunks[s][0])
        for s in [2, 1, 3] + [0]:
            wait = ahead if s == 3 else []
            part = field_chunk(scale, s, here, field_z, pieces[len(chunks[s]):], share_z, after + wait)
            after = [part]
            chunks[s].append(swap(part, "gy", s) if s else part)
    else:
        sketch = jnp.concatenate(pieces, axis=0) * scale
        raw = lax.dot_general(flat, sketch, dims(1, 1), precision=HIGH)
        raw = raw.reshape(planes * rows_y, rows_z, ranks_x)
        for s in order + [0]:
            chunk = lax.dynamic_slice_in_dim(raw, (gy ^ s) * share_z, share_z, 1)
            chunks[s] = swap(chunk, "gy", s) if s else chunk

    inverse_x = inverse_factor_x(scale, rank_x, quarter, pieces)
    factor_x = make_factor_x(scale, inverse_x, pieces)

    if tiled:
        slabs = [None] * n_gy
        after = []
        for s in [0] + order:
            slabs[s] = lift(planes, share_z, inverse_x, chunks[s], after)
            after = [slabs[s]]
        scratch = [pltpu.VMEM((all_rows_y, all_rows_y), jnp.float32)] * 2
        shape = (all_rows_y, ranks_y)
        part_y = kernel_call(gram_kernel, "gram", shape, [here], [omega_y.T] + slabs, scratch)
    else:
        spread = jnp.stack(chunks).reshape(-1, ranks_x)
        spread = lax.dot_general(spread, inverse_x, dims(1, 0), precision=HIGH)
        spread = spread.reshape(n_gy, planes, rows_y, share_z, ranks_x)
        local_gram_y = jnp.einsum("gvazr,hvbzr->gahb", spread, spread, precision=HIGH)
        local_gram_y = local_gram_y.reshape(all_rows_y, all_rows_y)
        omega_p = by_step(omega_y.reshape(n_gy, rows_y, ranks_y), gy, n_gy).reshape(all_rows_y, ranks_y)
        part_y = jnp.dot(local_gram_y, omega_p, precision=HIGHEST)
        part_y = by_step(part_y.reshape(n_gy, rows_y, ranks_y), gy, n_gy).reshape(all_rows_y, ranks_y)
    for axis in ("vert", "gz"):
        count = lax.axis_size(axis)
        got = [swap(part_y, axis, s) for s in steps(count)]
        for other in got:
            part_y = part_y + other
    parts = [part_y] + [swap(part_y, "gy", s) for s in steps(n_gy)]
    factor_y = make_factor_y(rank_y, parts, float(all_planes * all_rows_z * ranks_x))

    if tiled:
        shape = (planes, share_k, share_z, ranks_x)
        scratch = [pltpu.VMEM((ranks_y, planes * share_z * ranks_x), jnp.float32)]

        which = steps(n_gy) + [0]
        kernel = functools.partial(mix_kernel, which)
        blocks = kernel_call(kernel, "mix", [shape] * n_gy, [here], [factor_y] + slabs, scratch)
        pieces = [None] * n_gy
        for s, block in zip(which, blocks):
            pieces[s] = swap(block, "gy", s) if s else block
        core = place(here, pieces, (planes, share_k, rows_z, ranks_x))
        return (core, factor_x, factor_y)
    weights = by_step(factor_y.reshape(n_gy, rows_y, ranks_y), gy, n_gy)
    weights = weights.reshape(n_gy, rows_y, n_gy, share_k)
    weights = jnp.moveaxis(by_step(jnp.moveaxis(weights, 2, 0), gy, n_gy), 0, 2)
    mixed = jnp.einsum("gvyzr,gyhk->hvkzr", spread, weights, precision=HIGH)
    pieces = [None] * n_gy
    for s in steps(n_gy):
        pieces[s] = swap(mixed[s], "gy", s)
    pieces[0] = mixed[0]
    core = by_step(jnp.stack(pieces), gy, n_gy)
    core = jnp.moveaxis(core, 0, 2).reshape(planes, share_k, rows_z, ranks_x)
    return (core, factor_x, factor_y)


def solution(mesh):
    in_specs = (P(("grp", "vert"), "gy", "gz", None), P(), P(), P("grp"), P("grp"))
    out_specs = (P(("grp", "vert"), "gy", "gz", None), P("grp", None), P("grp", None))
    return jax.shard_map(body, mesh=mesh, in_specs=in_specs, out_specs=out_specs, check_vma=False)
```

```python
import functools

import jax
import jax.numpy as jnp
from jax import lax
from jax.experimental import pallas as pl
from jax.experimental.pallas import tpu as pltpu
from jax.sharding import PartitionSpec as P

HIGH = lax.Precision.HIGH
HIGHEST = lax.Precision.HIGHEST


def swap(value, axes, step):
    count = lax.axis_size(axes)
    assert count & (count - 1) == 0
    return lax.ppermute(value, axes, [(i, i ^ step) for i in range(count)])


def steps(count):
    return sorted(range(1, count), key=lambda s: (s % 4 != 2, s))


def by_step(blocks, me, count):
    if count == 4:
        pairs = blocks.reshape((2, 2) + blocks.shape[1:])
        pairs = jnp.where(me & 2 != 0, pairs[::-1], pairs)
        pairs = jnp.where(me & 1 != 0, pairs[:, ::-1], pairs)
        return pairs.reshape(blocks.shape)
    return jnp.take(blocks, me ^ jnp.arange(count), axis=0)


def sum_over_gy(part):
    count = lax.axis_size("gy")
    got = [swap(part, "gy", s) for s in ((3, 1, 2) if count == 4 else steps(count))]
    for other in got:
        part = part + other
    return part


def sum_sketch(parts):
    cores = lax.axis_size("vert")
    count = lax.axis_size("gz")
    sums = []
    for z in [*steps(count), 0]:
        total = parts[z * cores]
        for v in steps(cores):
            total = total + swap(parts[z * cores + v], "vert", v)
        sums.append(swap(total, "gz", z) if z else total)
    mine = sums[-1]
    for other in sums[:-1]:
        mine = mine + other
    mine = sum_over_gy(mine)
    return [mine] + [swap(mine, ("gz", "vert"), k) for k in range(1, count * cores)]


def dims(left, right):
    return (((left,), (right,)), ((), ()))


def mxu(a, b, numbers):
    return lax.dot_general(a, b, numbers, preferred_element_type=jnp.float32)


def exact(a, b, numbers):
    return lax.dot_general(a, b, numbers, precision=HIGHEST, preferred_element_type=jnp.float32)


def halves(value):
    high = value.astype(jnp.bfloat16)
    return high, (value - high.astype(jnp.float32)).astype(jnp.bfloat16)


VMEM = pl.BlockSpec(memory_space=pltpu.VMEM)
SMEM = pl.BlockSpec(memory_space=pltpu.SMEM)


def held(value):
    return pltpu.with_memory_space_constraint(value, pltpu.VMEM)


def kernel_call(body, name, out_shape, scalars, values, scratch=(), limit=16, whole_out=False):
    many = isinstance(out_shape, list)
    shapes = out_shape if many else [out_shape]
    if whole_out:
        outs = [jax.ShapeDtypeStruct(shape, jnp.float32) for shape in shapes]
    else:
        outs = [pltpu.VMEM(shape, jnp.float32) for shape in shapes]
    return pl.pallas_call(
        body,
        in_specs=[SMEM] * len(scalars) + [VMEM] * len(values),
        out_specs=[VMEM] * len(outs) if many else VMEM,
        out_shape=outs if many else outs[0],
        scratch_shapes=list(scratch),
        compiler_params=pltpu.CompilerParams(vmem_limit_bytes=limit << 20),
        name=name,
    )(*scalars, *[held(value) for value in values])


PIECES = 3


def sketch_kernel(me_ref, here_ref, field_hbm, omega_hbm, field_ref, *refs):
    *part_refs, omega_ref, total, arrived = refs
    omega_copy = pltpu.make_async_copy(omega_hbm, omega_ref, arrived.at[PIECES])
    omega_copy.start()
    width = omega_ref.shape[1]
    eighth = field_ref.shape[0] // 8
    ends = [0, 2 * eighth, 5 * eighth, 8 * eighth]
    copies = []
    for i in range(PIECES):
        rows = pl.ds(ends[i], ends[i + 1] - ends[i])
        copies.append(pltpu.make_async_copy(field_hbm.at[rows], field_ref.at[rows], arrived.at[i]))
        copies[i].start()
    omega_copy.wait()
    omega_high, omega_low = halves(omega_ref[...])
    omega_both = jnp.concatenate([omega_high, omega_low], axis=1)
    wide = narrow = None
    for i in range(PIECES):
        copies[i].wait()
        high, low = halves(field_ref[ends[i]:ends[i + 1], :])
        both = mxu(high, omega_both, dims(1, 0))
        projected = both[:, :width] + (both[:, width:] + mxu(low, omega_high, dims(1, 0)))
        proj_high, proj_low = halves(projected)
        first = mxu(jnp.concatenate([proj_high, proj_low], axis=1), high, dims(0, 0))
        second = mxu(proj_high, low, dims(0, 0))
        wide = first if wide is None else wide + first
        narrow = second if narrow is None else narrow + second
    total[...] = wide[:width, :] + (wide[width:, :] + narrow)
    share = width // len(part_refs)
    for k, ref in enumerate(part_refs):
        start = pl.multiple_of((me_ref[0] ^ k) * share, share)
        ref[...] = total[pl.ds(start, share), :]


def sketch_parts(me, here, count, flat, omega):
    rows, cells = flat.shape
    width = omega.shape[1]
    far = pl.BlockSpec(memory_space=pltpu.HBM)
    out = pl.pallas_call(
        sketch_kernel,
        in_specs=[SMEM, SMEM, far, far],
        out_specs=[VMEM] * (1 + count),
        out_shape=[pltpu.VMEM((rows, cells), jnp.float32)]
        + [pltpu.VMEM((width // count, cells), jnp.float32)] * count,
        scratch_shapes=[
            pltpu.VMEM((cells, width), jnp.float32),
            pltpu.VMEM((width, cells), jnp.float32),
            pltpu.SemaphoreType.DMA((PIECES + 1,)),
        ],
        compiler_params=pltpu.CompilerParams(vmem_limit_bytes=24 << 20),
        name="sketch",
    )(me, here, *[pltpu.with_memory_space_constraint(x, pltpu.HBM) for x in (flat, omega)])
    return out[0], out[1:]


def gather_sketch(scale, me_ref, piece_refs, whole):
    share = piece_refs[0].shape[0]
    for k, ref in enumerate(piece_refs):
        start = pl.multiple_of((me_ref[0] ^ k) * share, share)
        whole[pl.ds(start, share), :] = ref[...] * scale
    return whole[...]


def chunk_kernel(scale, step, many, here_ref, field_ref, *refs):
    piece_refs, out_ref = refs[:many], refs[-1]
    sketch = jnp.concatenate([ref[...] for ref in piece_refs], axis=0) * scale
    count = sketch.shape[0]
    rows, _, cells = field_ref.shape
    share = out_ref.shape[1] // rows
    start = pl.multiple_of((here_ref[0] ^ step) * share, share)
    high, low = halves(field_ref[:, pl.ds(start, share), :].reshape(rows * share, cells))
    sketch_high, sketch_low = halves(sketch)
    both = mxu(jnp.concatenate([sketch_high, sketch_low], axis=0), high, dims(1, 1))
    out_ref[...] = both[:count] + (both[count:] + mxu(sketch_high, low, dims(1, 1)))


def field_chunk(scale, step, here, field, pieces, share, after):
    kernel = functools.partial(chunk_kernel, scale, step, len(pieces))
    shape = (sum(piece.shape[0] for piece in pieces), field.shape[0] * share)
    return kernel_call(kernel, "chunk", shape, [here], [field] + pieces + after)


def lift_kernel(planes, share, count, inverse_ref, *refs):
    out_ref = refs[-1]
    inv_high, inv_low = halves(inverse_ref[...])
    width = inv_high.shape[1]
    high, low = halves(jnp.concatenate([ref[...] for ref in refs[:count]], axis=0))
    both = mxu(high, jnp.concatenate([inv_high, inv_low], axis=1), dims(0, 0))
    value = both[:, :width] + (both[:, width:] + mxu(low, inv_high, dims(0, 0)))
    value = jnp.swapaxes(value.reshape(planes, out_ref.shape[0], share, width), 1, 2)
    for v in range(planes):
        for z in range(share):
            at = (v * share + z) * width
            out_ref[:, at:at + width] = value[v, z]


def lift(planes, share, inverse, chunk, after):
    samples, width = chunk[0].shape[1], inverse.shape[1]
    shape = (samples // (planes * share), planes * share * width)
    kernel = functools.partial(lift_kernel, planes, share, len(chunk))
    return kernel_call(kernel, "lift", shape, [], [inverse] + chunk + after)


def gram_kernel(me_ref, omega_ref, *refs):
    *slab_refs, part_ref, rows_ref, cols_ref = refs
    share = slab_refs[0].shape[0]
    high, low = halves(jnp.concatenate([ref[...] for ref in slab_refs], axis=0))
    rows_ref[...] = mxu(high, high, dims(1, 1)) + (mxu(high, low, dims(1, 1)) + mxu(low, high, dims(1, 1)))
    for ref, out in ((rows_ref, cols_ref), (cols_ref, rows_ref)):
        value = ref[...].T
        for k in range(len(slab_refs)):
            start = pl.multiple_of((me_ref[0] ^ k) * share, share)
            out[pl.ds(start, share), :] = value[k * share:(k + 1) * share, :]
    part_ref[...] = exact(rows_ref[...], omega_ref[...], dims(1, 1))


def mix_kernel(which, me_ref, factor_ref, *refs):
    count = factor_ref.shape[0] // refs[0].shape[0]
    slab_refs, out_refs, mixed = refs[:count], refs[-1 - len(which):-1], refs[-1]
    planes, share_k, share_z, width = out_refs[0].shape
    rows_y = slab_refs[0].shape[0]
    own = [factor_ref[pl.ds(pl.multiple_of((me_ref[0] ^ k) * rows_y, rows_y), rows_y), :] for k in range(count)]
    fac_high, fac_low = halves(jnp.concatenate(own, axis=0))
    high, low = halves(jnp.concatenate([ref[...] for ref in slab_refs], axis=0))
    mixed[...] = mxu(fac_high, high, dims(0, 0)) + (mxu(fac_high, low, dims(0, 0)) + mxu(fac_low, high, dims(0, 0)))
    for k, ref in zip(which, out_refs):
        start = pl.multiple_of((me_ref[0] ^ k) * share_k, share_k)
        block = mixed[pl.ds(start, share_k), :]
        for v in range(planes):
            at = lambda z: (v * share_z + z) * width
            rows = jnp.stack([block[:, at(z):at(z) + width] for z in range(share_z)], axis=0)
            ref[v] = jnp.swapaxes(rows, 0, 1)


def place_kernel(order, me_ref, *refs):
    *piece_refs, out_hbm, placed = refs
    share = piece_refs[0].shape[2]
    copies = []
    for k, ref in zip(order, piece_refs):
        start = pl.multiple_of((me_ref[0] ^ k) * share, share)
        copy = pltpu.make_async_copy(ref, out_hbm.at[:, :, pl.ds(start, share), :], placed.at[k])
        copy.start()
        copies.append(copy)
    for copy in copies:
        copy.wait()


def place(me, pieces, shape):
    order = steps(len(pieces)) + [0]
    return pl.pallas_call(
        functools.partial(place_kernel, order),
        in_specs=[SMEM] + [VMEM] * len(pieces),
        out_specs=pl.BlockSpec(memory_space=pltpu.HBM),
        out_shape=jax.ShapeDtypeStruct(shape, jnp.float32),
        scratch_shapes=[pltpu.SemaphoreType.DMA((len(pieces),))],
        compiler_params=pltpu.CompilerParams(vmem_limit_bytes=16 << 20),
        name="place",
    )(me, *[held(pieces[k]) for k in order])


def eliminate(gram, count, rank, out_ref):
    lanes = lax.broadcasted_iota(jnp.int32, (8, count), 1)
    subs = lax.broadcasted_iota(jnp.int32, (8, count), 0)
    blocks = count // 8
    full = lambda x: jnp.broadcast_to(x, (8, count))
    left = [gram[8 * b:8 * b + 8, :] for b in range(blocks)]
    right = [(lanes == subs + 8 * b).astype(jnp.float32) for b in range(blocks)]
    for b in range(blocks):
        at = 8 * b
        l = [full(left[b][k:k + 1, :]) for k in range(8)]
        r = [full(right[b][k:k + 1, :]) for k in range(8)]
        a = {(k, m): full(l[k][:, at + m:at + m + 1]) for k in range(8) for m in range(k, 8)}
        inv, f = {}, {}
        for k in range(8):
            inv[k] = 1.0 / a[k, k]
            for m in range(k + 1, 8):
                f[k, m] = a[k, m] * inv[k]
                for q in range(m, 8):
                    a[m, q] = a[m, q] - f[k, m] * a[k, q]
                l[m] = l[m] - f[k, m] * l[k]
                r[m] = r[m] - f[k, m] * r[k]
            row = (r[k] * lax.rsqrt(a[k, k]))[0:1]
            out_ref[at + k:at + k + 1, :] = jnp.where(at + k < rank, row, 0.0)
        if b + 1 == blocks:
            break
        w, v = {}, {}
        for k in reversed(range(8)):
            w[k], v[k] = l[k] * inv[k], r[k] * inv[k]
            for m in range(k + 1, 8):
                w[k] = w[k] - f[k, m] * w[m]
                v[k] = v[k] - f[k, m] * v[m]
        for i in range(b + 1, blocks):
            column = [full(left[i][:, at + k:at + k + 1]) for k in range(8)]
            for k in range(8):
                left[i] = left[i] - column[k] * w[k]
                right[i] = right[i] - column[k] * v[k]


def factor_x_kernel(scale, rank_ref, me_ref, *refs):
    *piece_refs, out_ref, sketch_ref, inverse_ref = refs
    sketch_t = gather_sketch(scale, me_ref, piece_refs, sketch_ref)
    eliminate(exact(sketch_t, sketch_t, dims(1, 1)), sketch_t.shape[0], rank_ref[0], inverse_ref)
    inverse_ref[...] = inverse_ref[...].T
    share = piece_refs[0].shape[0]
    for k in range(len(piece_refs)):
        start = pl.multiple_of((me_ref[0] ^ k) * share, share)
        out_ref[k * share:(k + 1) * share, :] = inverse_ref[pl.ds(start, share), :]


def inverse_factor_x(scale, rank, me, pieces):
    width = pieces[0].shape[0] * len(pieces)
    scratch = [pltpu.VMEM((width, pieces[0].shape[1]), jnp.float32), pltpu.VMEM((width, width), jnp.float32)]
    kernel = functools.partial(factor_x_kernel, scale)
    return kernel_call(kernel, "factor_x", (width, width), [rank, me], pieces, scratch)


def apply_kernel(scale, inverse_ref, *refs):
    *piece_refs, out_ref = refs
    sketch = jnp.concatenate([ref[...] for ref in piece_refs], axis=0) * scale
    out_ref[...] = exact(sketch, inverse_ref[...], dims(0, 0))


def make_factor_x(scale, inverse, pieces):
    shape = (pieces[0].shape[1], inverse.shape[1])
    kernel = functools.partial(apply_kernel, scale)
    return kernel_call(kernel, "apply", shape, [], [inverse] + pieces, whole_out=True)


def factor_y_kernel(divisor, rank_ref, *refs):
    *part_refs, out_ref, inverse = refs
    sketch = part_refs[0][...]
    for ref in part_refs[1:]:
        sketch = sketch + ref[...]
    sketch = sketch / divisor
    eliminate(exact(sketch, sketch, dims(0, 0)), sketch.shape[1], rank_ref[0], inverse)
    out_ref[...] = exact(sketch, inverse[...], dims(1, 1))


def make_factor_y(rank, parts, divisor):
    width = parts[0].shape[1]
    scratch = [pltpu.VMEM((width, width), jnp.float32)]
    kernel = functools.partial(factor_y_kernel, divisor)
    return kernel_call(kernel, "factor_y", parts[0].shape, [rank], parts, scratch)


def body(field, omega_x, omega_y, rank_x, rank_y):
    planes, rows_y, rows_z, cells_x = field.shape
    ranks_x = omega_x.shape[1]
    ranks_y = omega_y.shape[1]
    n_gy = lax.axis_size("gy")
    gy = lax.axis_index("gy")
    all_planes = planes * lax.axis_size("vert")
    all_rows_y = rows_y * n_gy
    all_rows_z = rows_z * lax.axis_size("gz")
    flat = field.reshape(-1, cells_x)

    here = gy[None].astype(jnp.int32)
    quarter = lax.axis_index("gz") * lax.axis_size("vert") + lax.axis_index("vert")
    n_quarter = lax.axis_size(("gz", "vert"))
    quarter = quarter[None].astype(jnp.int32)
    field_v, parts = sketch_parts(quarter, here, n_quarter, flat, omega_x)
    pieces = sum_sketch(parts)
    scale = 1.0 / float(all_planes * all_rows_y * all_rows_z)

    share_z = rows_z // n_gy
    share_k = ranks_y // n_gy
    field_z = field_v.reshape(planes * rows_y, rows_z, cells_x)
    tiled = share_z % 8 == 0 and share_k % 8 == 0 and n_gy == 4 and n_quarter == 4
    inverse_x = inverse_factor_x(scale, rank_x, quarter, pieces)
    order = steps(n_gy)
    chunks = [[] for _ in range(n_gy)]
    if tiled:
        after, ahead = [], []
        for s in order:
            if s & 2:
                part = field_chunk(scale, s, here, field_z, pieces[:2], share_z, after)
                after = [part]
                chunks[s].append(swap(part, "gy", s))
                ahead.append(chunks[s][0])
        for s in [2, 1, 0, 3]:
            wait = ahead + [inverse_x] if s == 3 else []
            part = field_chunk(scale, s, here, field_z, pieces[2 * len(chunks[s]):], share_z, after + wait)
            after = [part]
            chunks[s].append(swap(part, "gy", s) if s else part)
    else:
        sketch = jnp.concatenate(pieces, axis=0) * scale
        raw = lax.dot_general(flat, sketch, dims(1, 1), precision=HIGH)
        raw = raw.reshape(planes * rows_y, rows_z, ranks_x)
        for s in order + [0]:
            chunk = lax.dynamic_slice_in_dim(raw, (gy ^ s) * share_z, share_z, 1)
            chunks[s] = swap(chunk, "gy", s) if s else chunk

    factor_x = make_factor_x(scale, inverse_x, pieces)

    if tiled:
        slabs = [None] * n_gy
        after = []
        for s in [0] + order:
            slabs[s] = lift(planes, share_z, inverse_x, chunks[s], after)
            after = [slabs[s]]
        scratch = [pltpu.VMEM((all_rows_y, all_rows_y), jnp.float32)] * 2
        shape = (all_rows_y, ranks_y)
        part_y = kernel_call(gram_kernel, "gram", shape, [here], [omega_y.T] + slabs, scratch)
    else:
        spread = jnp.stack(chunks).reshape(-1, ranks_x)
        spread = lax.dot_general(spread, inverse_x, dims(1, 0), precision=HIGH)
        spread = spread.reshape(n_gy, planes, rows_y, share_z, ranks_x)
        local_gram_y = jnp.einsum("gvazr,hvbzr->gahb", spread, spread, precision=HIGH)
        local_gram_y = local_gram_y.reshape(all_rows_y, all_rows_y)
        omega_p = by_step(omega_y.reshape(n_gy, rows_y, ranks_y), gy, n_gy).reshape(all_rows_y, ranks_y)
        part_y = jnp.dot(local_gram_y, omega_p, precision=HIGHEST)
        part_y = by_step(part_y.reshape(n_gy, rows_y, ranks_y), gy, n_gy).reshape(all_rows_y, ranks_y)
    for axis in ("vert", "gz"):
        count = lax.axis_size(axis)
        got = [swap(part_y, axis, s) for s in steps(count)]
        for other in got:
            part_y = part_y + other
    parts = [part_y] + [swap(part_y, "gy", s) for s in range(1, n_gy)]
    factor_y = make_factor_y(rank_y, parts, float(all_planes * all_rows_z * ranks_x))

    if tiled:
        shape = (planes, share_k, share_z, ranks_x)
        scratch = [pltpu.VMEM((ranks_y, planes * share_z * ranks_x), jnp.float32)]

        which = steps(n_gy) + [0]
        kernel = functools.partial(mix_kernel, which)
        blocks = kernel_call(kernel, "mix", [shape] * n_gy, [here], [factor_y] + slabs, scratch)
        pieces = [None] * n_gy
        for s, block in zip(which, blocks):
            pieces[s] = swap(block, "gy", s) if s else block
        core = place(here, pieces, (planes, share_k, rows_z, ranks_x))
        return (core, factor_x, factor_y)
    weights = by_step(factor_y.reshape(n_gy, rows_y, ranks_y), gy, n_gy)
    weights = weights.reshape(n_gy, rows_y, n_gy, share_k)
    weights = jnp.moveaxis(by_step(jnp.moveaxis(weights, 2, 0), gy, n_gy), 0, 2)
    mixed = jnp.einsum("gvyzr,gyhk->hvkzr", spread, weights, precision=HIGH)
    pieces = [None] * n_gy
    for s in steps(n_gy):
        pieces[s] = swap(mixed[s], "gy", s)
    pieces[0] = mixed[0]
    core = by_step(jnp.stack(pieces), gy, n_gy)
    core = jnp.moveaxis(core, 0, 2).reshape(planes, share_k, rows_z, ranks_x)
    return (core, factor_x, factor_y)


def solution(mesh):
    in_specs = (P(("grp", "vert"), "gy", "gz", None), P(), P(), P("grp"), P("grp"))
    out_specs = (P(("grp", "vert"), "gy", "gz", None), P("grp", None), P("grp", None))
    return jax.shard_map(body, mesh=mesh, in_specs=in_specs, out_specs=out_specs, check_vma=False)
```

```python
import functools

import jax
import jax.numpy as jnp
from jax import lax
from jax.experimental import pallas as pl
from jax.experimental.pallas import tpu as pltpu
from jax.sharding import PartitionSpec as P

HIGHEST = lax.Precision.HIGHEST


def swap(value, axes, step):
    count = lax.axis_size(axes)
    assert count & (count - 1) == 0
    return lax.ppermute(value, axes, [(i, i ^ step) for i in range(count)])


def steps(count):
    return sorted(range(1, count), key=lambda s: (s % 4 != 2, s))


def by_step(blocks, me, count):
    if count == 4:
        pairs = blocks.reshape((2, 2) + blocks.shape[1:])
        pairs = jnp.where(me & 2 != 0, pairs[::-1], pairs)
        pairs = jnp.where(me & 1 != 0, pairs[:, ::-1], pairs)
        return pairs.reshape(blocks.shape)
    return jnp.take(blocks, me ^ jnp.arange(count), axis=0)


def sum_over_gy(part):
    count = lax.axis_size("gy")
    got = [swap(part, "gy", s) for s in steps(count)]
    for other in got:
        part = part + other
    return part


def sum_sketch(parts):
    cores = lax.axis_size("vert")
    count = lax.axis_size("gz")
    sums = []
    for z in [*steps(count), 0]:
        total = parts[z * cores]
        for v in steps(cores):
            total = total + swap(parts[z * cores + v], "vert", v)
        sums.append(swap(total, "gz", z) if z else total)
    mine = sums[-1]
    for other in sums[:-1]:
        mine = mine + other
    mine = sum_over_gy(mine)
    return [mine] + [swap(mine, ("gz", "vert"), k) for k in range(1, count * cores)]


def dims(left, right):
    return (((left,), (right,)), ((), ()))


def mxu(a, b, numbers):
    return lax.dot_general(a, b, numbers, preferred_element_type=jnp.float32)


def exact(a, b, numbers):
    return lax.dot_general(a, b, numbers, precision=HIGHEST, preferred_element_type=jnp.float32)


def halves(value):
    high = value.astype(jnp.bfloat16)
    return high, (value - high.astype(jnp.float32)).astype(jnp.bfloat16)


VMEM = pl.BlockSpec(memory_space=pltpu.VMEM)
SMEM = pl.BlockSpec(memory_space=pltpu.SMEM)


def held(value):
    return pltpu.with_memory_space_constraint(value, pltpu.VMEM)


def kernel_call(body, name, out_shape, scalars, values, scratch=(), limit=16, whole_out=False):
    many = isinstance(out_shape, list)
    shapes = out_shape if many else [out_shape]
    if whole_out:
        outs = [jax.ShapeDtypeStruct(shape, jnp.float32) for shape in shapes]
    else:
        outs = [pltpu.VMEM(shape, jnp.float32) for shape in shapes]
    return pl.pallas_call(
        body,
        in_specs=[SMEM] * len(scalars) + [VMEM] * len(values),
        out_specs=[VMEM] * len(outs) if many else VMEM,
        out_shape=outs if many else outs[0],
        scratch_shapes=list(scratch),
        compiler_params=pltpu.CompilerParams(vmem_limit_bytes=limit << 20),
        name=name,
    )(*scalars, *[held(value) for value in values])


PIECES = 3


def sketch_kernel(me_ref, here_ref, field_hbm, omega_hbm, field_ref, *refs):
    *part_refs, omega_ref, total, arrived = refs
    omega_copy = pltpu.make_async_copy(omega_hbm, omega_ref, arrived.at[PIECES])
    omega_copy.start()
    width = omega_ref.shape[1]
    eighth = field_ref.shape[0] // 8
    ends = [0, 2 * eighth, 5 * eighth, 8 * eighth]
    copies = []
    for i in range(PIECES):
        rows = pl.ds(ends[i], ends[i + 1] - ends[i])
        copies.append(pltpu.make_async_copy(field_hbm.at[rows], field_ref.at[rows], arrived.at[i]))
        copies[i].start()
    omega_copy.wait()
    omega_high, omega_low = halves(omega_ref[...])
    omega_both = jnp.concatenate([omega_high, omega_low], axis=1)
    wide = narrow = None
    for i in range(PIECES):
        copies[i].wait()
        high, low = halves(field_ref[ends[i]:ends[i + 1], :])
        both = mxu(high, omega_both, dims(1, 0))
        projected = both[:, :width] + (both[:, width:] + mxu(low, omega_high, dims(1, 0)))
        proj_high, proj_low = halves(projected)
        first = mxu(jnp.concatenate([proj_high, proj_low], axis=1), high, dims(0, 0))
        second = mxu(proj_high, low, dims(0, 0))
        wide = first if wide is None else wide + first
        narrow = second if narrow is None else narrow + second
    total[...] = wide[:width, :] + (wide[width:, :] + narrow)
    share = width // len(part_refs)
    for k, ref in enumerate(part_refs):
        start = pl.multiple_of((me_ref[0] ^ k) * share, share)
        ref[...] = total[pl.ds(start, share), :]


def sketch_parts(me, here, count, flat, omega):
    rows, cells = flat.shape
    width = omega.shape[1]
    far = pl.BlockSpec(memory_space=pltpu.HBM)
    out = pl.pallas_call(
        sketch_kernel,
        in_specs=[SMEM, SMEM, far, far],
        out_specs=[VMEM] * (1 + count),
        out_shape=[pltpu.VMEM((rows, cells), jnp.float32)]
        + [pltpu.VMEM((width // count, cells), jnp.float32)] * count,
        scratch_shapes=[
            pltpu.VMEM((cells, width), jnp.float32),
            pltpu.VMEM((width, cells), jnp.float32),
            pltpu.SemaphoreType.DMA((PIECES + 1,)),
        ],
        compiler_params=pltpu.CompilerParams(vmem_limit_bytes=24 << 20),
        name="sketch",
    )(me, here, *[pltpu.with_memory_space_constraint(x, pltpu.HBM) for x in (flat, omega)])
    return out[0], out[1:]


def gather_sketch(scale, me_ref, piece_refs, whole):
    share = piece_refs[0].shape[0]
    for k, ref in enumerate(piece_refs):
        start = pl.multiple_of((me_ref[0] ^ k) * share, share)
        whole[pl.ds(start, share), :] = ref[...] * scale
    return whole[...]


def chunk_kernel(scale, step, many, here_ref, field_ref, *refs):
    piece_refs, out_ref = refs[:many], refs[-1]
    sketch = jnp.concatenate([ref[...] for ref in piece_refs], axis=0) * scale
    count = sketch.shape[0]
    rows, _, cells = field_ref.shape
    share = out_ref.shape[1] // rows
    start = pl.multiple_of((here_ref[0] ^ step) * share, share)
    high, low = halves(field_ref[:, pl.ds(start, share), :].reshape(rows * share, cells))
    sketch_high, sketch_low = halves(sketch)
    both = mxu(jnp.concatenate([sketch_high, sketch_low], axis=0), high, dims(1, 1))
    out_ref[...] = both[:count] + (both[count:] + mxu(sketch_high, low, dims(1, 1)))


def field_chunk(scale, step, here, field, pieces, share, after):
    kernel = functools.partial(chunk_kernel, scale, step, len(pieces))
    shape = (sum(piece.shape[0] for piece in pieces), field.shape[0] * share)
    return kernel_call(kernel, "chunk", shape, [here], [field] + pieces + after)


def lift_kernel(planes, share, count, inverse_ref, *refs):
    out_ref = refs[-1]
    inv_high, inv_low = halves(inverse_ref[...])
    width = inv_high.shape[1]
    high, low = halves(jnp.concatenate([ref[...] for ref in refs[:count]], axis=0))
    both = mxu(high, jnp.concatenate([inv_high, inv_low], axis=1), dims(0, 0))
    value = both[:, :width] + (both[:, width:] + mxu(low, inv_high, dims(0, 0)))
    value = jnp.swapaxes(value.reshape(planes, out_ref.shape[0], share, width), 1, 2)
    for v in range(planes):
        for z in range(share):
            at = (v * share + z) * width
            out_ref[:, at:at + width] = value[v, z]


def lift(planes, share, inverse, chunk, after):
    samples, width = chunk[0].shape[1], inverse.shape[1]
    shape = (samples // (planes * share), planes * share * width)
    kernel = functools.partial(lift_kernel, planes, share, len(chunk))
    return kernel_call(kernel, "lift", shape, [], [inverse] + chunk + after)


def gram_kernel(me_ref, omega_ref, *refs):
    *slab_refs, part_ref, rows_ref, cols_ref = refs
    share = slab_refs[0].shape[0]
    high, low = halves(jnp.concatenate([ref[...] for ref in slab_refs], axis=0))
    rows_ref[...] = mxu(high, high, dims(1, 1)) + (mxu(high, low, dims(1, 1)) + mxu(low, high, dims(1, 1)))
    for ref, out in ((rows_ref, cols_ref), (cols_ref, rows_ref)):
        value = ref[...].T
        for k in range(len(slab_refs)):
            start = pl.multiple_of((me_ref[0] ^ k) * share, share)
            out[pl.ds(start, share), :] = value[k * share:(k + 1) * share, :]
    part_ref[...] = exact(rows_ref[...], omega_ref[...], dims(1, 1))


def mix_kernel(which, me_ref, factor_ref, *refs):
    count = factor_ref.shape[0] // refs[0].shape[0]
    slab_refs, out_refs, mixed = refs[:count], refs[-1 - len(which):-1], refs[-1]
    planes, share_k, share_z, width = out_refs[0].shape
    rows_y = slab_refs[0].shape[0]
    own = [factor_ref[pl.ds(pl.multiple_of((me_ref[0] ^ k) * rows_y, rows_y), rows_y), :] for k in range(count)]
    fac_high, fac_low = halves(jnp.concatenate(own, axis=0))
    high, low = halves(jnp.concatenate([ref[...] for ref in slab_refs], axis=0))
    mixed[...] = mxu(fac_high, high, dims(0, 0)) + (mxu(fac_high, low, dims(0, 0)) + mxu(fac_low, high, dims(0, 0)))
    for k, ref in zip(which, out_refs):
        start = pl.multiple_of((me_ref[0] ^ k) * share_k, share_k)
        block = mixed[pl.ds(start, share_k), :]
        for v in range(planes):
            at = lambda z: (v * share_z + z) * width
            rows = jnp.stack([block[:, at(z):at(z) + width] for z in range(share_z)], axis=0)
            ref[v] = jnp.swapaxes(rows, 0, 1)


def place_kernel(order, me_ref, *refs):
    *piece_refs, out_hbm, placed = refs
    share = piece_refs[0].shape[2]
    copies = []
    for k, ref in zip(order, piece_refs):
        start = pl.multiple_of((me_ref[0] ^ k) * share, share)
        copy = pltpu.make_async_copy(ref, out_hbm.at[:, :, pl.ds(start, share), :], placed.at[k])
        copy.start()
        copies.append(copy)
    for copy in copies:
        copy.wait()


def place(me, pieces, shape):
    order = steps(len(pieces)) + [0]
    return pl.pallas_call(
        functools.partial(place_kernel, order),
        in_specs=[SMEM] + [VMEM] * len(pieces),
        out_specs=pl.BlockSpec(memory_space=pltpu.HBM),
        out_shape=jax.ShapeDtypeStruct(shape, jnp.float32),
        scratch_shapes=[pltpu.SemaphoreType.DMA((len(pieces),))],
        compiler_params=pltpu.CompilerParams(vmem_limit_bytes=16 << 20),
        name="place",
    )(me, *[held(pieces[k]) for k in order])


def eliminate(gram, count, rank, out_ref):
    lanes = lax.broadcasted_iota(jnp.int32, (8, count), 1)
    subs = lax.broadcasted_iota(jnp.int32, (8, count), 0)
    blocks = count // 8
    full = lambda x: jnp.broadcast_to(x, (8, count))
    left = [gram[8 * b:8 * b + 8, :] for b in range(blocks)]
    right = [(lanes == subs + 8 * b).astype(jnp.float32) for b in range(blocks)]
    for b in range(blocks):
        at = 8 * b
        l = [full(left[b][k:k + 1, :]) for k in range(8)]
        r = [full(right[b][k:k + 1, :]) for k in range(8)]
        a = {(k, m): full(l[k][:, at + m:at + m + 1]) for k in range(8) for m in range(k, 8)}
        inv, f = {}, {}
        for k in range(8):
            inv[k] = 1.0 / a[k, k]
            for m in range(k + 1, 8):
                f[k, m] = a[k, m] * inv[k]
                for q in range(m, 8):
                    a[m, q] = a[m, q] - f[k, m] * a[k, q]
                l[m] = l[m] - f[k, m] * l[k]
                r[m] = r[m] - f[k, m] * r[k]
            row = (r[k] * lax.rsqrt(a[k, k]))[0:1]
            out_ref[at + k:at + k + 1, :] = jnp.where(at + k < rank, row, 0.0)
        if b + 1 == blocks:
            break
        w, v = {}, {}
        for k in reversed(range(8)):
            w[k], v[k] = l[k] * inv[k], r[k] * inv[k]
            for m in range(k + 1, 8):
                w[k] = w[k] - f[k, m] * w[m]
                v[k] = v[k] - f[k, m] * v[m]
        for i in range(b + 1, blocks):
            column = [full(left[i][:, at + k:at + k + 1]) for k in range(8)]
            for k in range(8):
                left[i] = left[i] - column[k] * w[k]
                right[i] = right[i] - column[k] * v[k]


def factor_x_kernel(scale, rank_ref, me_ref, *refs):
    *piece_refs, out_ref, sketch_ref, inverse_ref = refs
    sketch_t = gather_sketch(scale, me_ref, piece_refs, sketch_ref)
    eliminate(exact(sketch_t, sketch_t, dims(1, 1)), sketch_t.shape[0], rank_ref[0], inverse_ref)
    inverse_ref[...] = inverse_ref[...].T
    share = piece_refs[0].shape[0]
    for k in range(len(piece_refs)):
        start = pl.multiple_of((me_ref[0] ^ k) * share, share)
        out_ref[k * share:(k + 1) * share, :] = inverse_ref[pl.ds(start, share), :]


def inverse_factor_x(scale, rank, me, pieces):
    width = pieces[0].shape[0] * len(pieces)
    scratch = [pltpu.VMEM((width, pieces[0].shape[1]), jnp.float32), pltpu.VMEM((width, width), jnp.float32)]
    kernel = functools.partial(factor_x_kernel, scale)
    return kernel_call(kernel, "factor_x", (width, width), [rank, me], pieces, scratch)


def apply_kernel(scale, inverse_ref, *refs):
    *piece_refs, out_ref = refs
    sketch = jnp.concatenate([ref[...] for ref in piece_refs], axis=0) * scale
    out_ref[...] = exact(sketch, inverse_ref[...], dims(0, 0))


def make_factor_x(scale, inverse, pieces):
    shape = (pieces[0].shape[1], inverse.shape[1])
    kernel = functools.partial(apply_kernel, scale)
    return kernel_call(kernel, "apply", shape, [], [inverse] + pieces, whole_out=True)


def factor_y_kernel(divisor, rank_ref, *refs):
    *part_refs, out_ref, inverse = refs
    sketch = part_refs[0][...]
    for ref in part_refs[1:]:
        sketch = sketch + ref[...]
    sketch = sketch / divisor
    eliminate(exact(sketch, sketch, dims(0, 0)), sketch.shape[1], rank_ref[0], inverse)
    out_ref[...] = exact(sketch, inverse[...], dims(1, 1))


def make_factor_y(rank, parts, divisor):
    width = parts[0].shape[1]
    scratch = [pltpu.VMEM((width, width), jnp.float32)]
    kernel = functools.partial(factor_y_kernel, divisor)
    return kernel_call(kernel, "factor_y", parts[0].shape, [rank], parts, scratch)


def body(field, omega_x, omega_y, rank_x, rank_y):
    planes, rows_y, rows_z, cells_x = field.shape
    ranks_x = omega_x.shape[1]
    ranks_y = omega_y.shape[1]
    n_gy = lax.axis_size("gy")
    gy = lax.axis_index("gy")
    all_planes = planes * lax.axis_size("vert")
    all_rows_y = rows_y * n_gy
    all_rows_z = rows_z * lax.axis_size("gz")
    flat = field.reshape(-1, cells_x)

    here = gy[None].astype(jnp.int32)
    quarter = lax.axis_index("gz") * lax.axis_size("vert") + lax.axis_index("vert")
    n_quarter = lax.axis_size(("gz", "vert"))
    quarter = quarter[None].astype(jnp.int32)
    field_v, parts = sketch_parts(quarter, here, n_quarter, flat, omega_x)
    pieces = sum_sketch(parts)
    scale = 1.0 / float(all_planes * all_rows_y * all_rows_z)

    share_z = rows_z // n_gy
    share_k = ranks_y // n_gy
    field_z = field_v.reshape(planes * rows_y, rows_z, cells_x)
    tiled = share_z % 8 == 0 and share_k % 8 == 0 and n_gy == 4 and n_quarter == 4
    inverse_x = inverse_factor_x(scale, rank_x, quarter, pieces)
    order = steps(n_gy)
    chunks = [[] for _ in range(n_gy)]
    if tiled:
        after, ahead = [], []
        for s in order:
            if s & 2:
                part = field_chunk(scale, s, here, field_z, pieces[:2], share_z, after)
                after = [part]
                chunks[s].append(swap(part, "gy", s))
                ahead.append(chunks[s][0])
        for s in [2, 1, 0, 3]:
            wait = ahead + [inverse_x] if s == 3 else []
            part = field_chunk(scale, s, here, field_z, pieces[2 * len(chunks[s]):], share_z, after + wait)
            after = [part]
            chunks[s].append(swap(part, "gy", s) if s else part)
    else:
        sketch = jnp.concatenate(pieces, axis=0) * scale
        raw = lax.dot_general(flat, sketch, dims(1, 1), precision=HIGHEST)
        raw = raw.reshape(planes * rows_y, rows_z, ranks_x)
        for s in order + [0]:
            chunk = lax.dynamic_slice_in_dim(raw, (gy ^ s) * share_z, share_z, 1)
            chunks[s] = swap(chunk, "gy", s) if s else chunk

    factor_x = make_factor_x(scale, inverse_x, pieces)

    if tiled:
        slabs = [None] * n_gy
        after = []
        for s in [0] + order:
            slabs[s] = lift(planes, share_z, inverse_x, chunks[s], after)
            after = [slabs[s]]
        scratch = [pltpu.VMEM((all_rows_y, all_rows_y), jnp.float32)] * 2
        shape = (all_rows_y, ranks_y)
        part_y = kernel_call(gram_kernel, "gram", shape, [here], [omega_y.T] + slabs, scratch)
    else:
        spread = jnp.stack(chunks).reshape(-1, ranks_x)
        spread = lax.dot_general(spread, inverse_x, dims(1, 0), precision=HIGHEST)
        spread = spread.reshape(n_gy, planes, rows_y, share_z, ranks_x)
        local_gram_y = jnp.einsum("gvazr,hvbzr->gahb", spread, spread, precision=HIGHEST)
        local_gram_y = local_gram_y.reshape(all_rows_y, all_rows_y)
        omega_p = by_step(omega_y.reshape(n_gy, rows_y, ranks_y), gy, n_gy).reshape(all_rows_y, ranks_y)
        part_y = jnp.dot(local_gram_y, omega_p, precision=HIGHEST)
        part_y = by_step(part_y.reshape(n_gy, rows_y, ranks_y), gy, n_gy).reshape(all_rows_y, ranks_y)
    for axis in ("vert", "gz"):
        count = lax.axis_size(axis)
        got = [swap(part_y, axis, s) for s in steps(count)]
        for other in got:
            part_y = part_y + other
    parts = [part_y] + [swap(part_y, "gy", s) for s in range(1, n_gy)]
    factor_y = make_factor_y(rank_y, parts, float(all_planes * all_rows_z * ranks_x))

    if tiled:
        shape = (planes, share_k, share_z, ranks_x)
        scratch = [pltpu.VMEM((ranks_y, planes * share_z * ranks_x), jnp.float32)]

        which = steps(n_gy) + [0]
        kernel = functools.partial(mix_kernel, which)
        blocks = kernel_call(kernel, "mix", [shape] * n_gy, [here], [factor_y] + slabs, scratch)
        pieces = [None] * n_gy
        for s, block in zip(which, blocks):
            pieces[s] = swap(block, "gy", s) if s else block
        core = place(here, pieces, (planes, share_k, rows_z, ranks_x))
        return (core, factor_x, factor_y)
    weights = by_step(factor_y.reshape(n_gy, rows_y, ranks_y), gy, n_gy)
    weights = weights.reshape(n_gy, rows_y, n_gy, share_k)
    weights = jnp.moveaxis(by_step(jnp.moveaxis(weights, 2, 0), gy, n_gy), 0, 2)
    mixed = jnp.einsum("gvyzr,gyhk->hvkzr", spread, weights, precision=HIGHEST)
    pieces = [None] * n_gy
    for s in steps(n_gy):
        pieces[s] = swap(mixed[s], "gy", s)
    pieces[0] = mixed[0]
    core = by_step(jnp.stack(pieces), gy, n_gy)
    core = jnp.moveaxis(core, 0, 2).reshape(planes, share_k, rows_z, ranks_x)
    return (core, factor_x, factor_y)


def solution(mesh):
    in_specs = (P(("grp", "vert"), "gy", "gz", None), P(), P(), P("grp"), P("grp"))
    out_specs = (P(("grp", "vert"), "gy", "gz", None), P("grp", None), P("grp", None))
    return jax.shard_map(body, mesh=mesh, in_specs=in_specs, out_specs=out_specs, check_vma=False)
```

```python
import functools

import jax
import jax.numpy as jnp
from jax import lax
from jax.experimental import pallas as pl
from jax.experimental.pallas import tpu as pltpu
from jax.sharding import PartitionSpec as P

HIGHEST = lax.Precision.HIGHEST


def swap(value, axes, step):
    count = lax.axis_size(axes)
    assert count & (count - 1) == 0
    return lax.ppermute(value, axes, [(i, i ^ step) for i in range(count)])


def steps(count):
    return sorted(range(1, count), key=lambda s: (s % 4 != 2, s))


def by_step(blocks, me, count):
    if count == 4:
        pairs = blocks.reshape((2, 2) + blocks.shape[1:])
        pairs = jnp.where(me & 2 != 0, pairs[::-1], pairs)
        pairs = jnp.where(me & 1 != 0, pairs[:, ::-1], pairs)
        return pairs.reshape(blocks.shape)
    return jnp.take(blocks, me ^ jnp.arange(count), axis=0)


def sum_over_gy(part):
    count = lax.axis_size("gy")
    got = [swap(part, "gy", s) for s in steps(count)]
    for other in got:
        part = part + other
    return part


def sum_sketch(parts):
    cores = lax.axis_size("vert")
    count = lax.axis_size("gz")
    sums = []
    for z in [*steps(count), 0]:
        total = parts[z * cores]
        for v in steps(cores):
            total = total + swap(parts[z * cores + v], "vert", v)
        sums.append(swap(total, "gz", z) if z else total)
    mine = sums[-1]
    for other in sums[:-1]:
        mine = mine + other
    mine = sum_over_gy(mine)
    return [mine] + [swap(mine, ("gz", "vert"), k) for k in range(1, count * cores)]


def dims(left, right):
    return (((left,), (right,)), ((), ()))


def mxu(a, b, numbers):
    return lax.dot_general(a, b, numbers, preferred_element_type=jnp.float32)


def exact(a, b, numbers):
    return lax.dot_general(a, b, numbers, precision=HIGHEST, preferred_element_type=jnp.float32)


def halves(value):
    high = value.astype(jnp.bfloat16)
    return high, (value - high.astype(jnp.float32)).astype(jnp.bfloat16)


VMEM = pl.BlockSpec(memory_space=pltpu.VMEM)
SMEM = pl.BlockSpec(memory_space=pltpu.SMEM)


def held(value):
    return pltpu.with_memory_space_constraint(value, pltpu.VMEM)


def kernel_call(body, name, out_shape, scalars, values, scratch=(), limit=16, whole_out=False):
    many = isinstance(out_shape, list)
    shapes = out_shape if many else [out_shape]
    if whole_out:
        outs = [jax.ShapeDtypeStruct(shape, jnp.float32) for shape in shapes]
    else:
        outs = [pltpu.VMEM(shape, jnp.float32) for shape in shapes]
    return pl.pallas_call(
        body,
        in_specs=[SMEM] * len(scalars) + [VMEM] * len(values),
        out_specs=[VMEM] * len(outs) if many else VMEM,
        out_shape=outs if many else outs[0],
        scratch_shapes=list(scratch),
        compiler_params=pltpu.CompilerParams(vmem_limit_bytes=limit << 20),
        name=name,
    )(*scalars, *[held(value) for value in values])


PIECES = 3


def sketch_kernel(me_ref, here_ref, field_hbm, omega_hbm, field_ref, *refs):
    *part_refs, omega_ref, total, arrived = refs
    omega_copy = pltpu.make_async_copy(omega_hbm, omega_ref, arrived.at[PIECES])
    omega_copy.start()
    width = omega_ref.shape[1]
    eighth = field_ref.shape[0] // 8
    ends = [0, 2 * eighth, 5 * eighth, 8 * eighth]
    copies = []
    for i in range(PIECES):
        rows = pl.ds(ends[i], ends[i + 1] - ends[i])
        copies.append(pltpu.make_async_copy(field_hbm.at[rows], field_ref.at[rows], arrived.at[i]))
        copies[i].start()
    omega_copy.wait()
    omega_high, omega_low = halves(omega_ref[...])
    omega_both = jnp.concatenate([omega_high, omega_low], axis=1)
    wide = narrow = None
    for i in range(PIECES):
        copies[i].wait()
        high, low = halves(field_ref[ends[i]:ends[i + 1], :])
        both = mxu(high, omega_both, dims(1, 0))
        projected = both[:, :width] + (both[:, width:] + mxu(low, omega_high, dims(1, 0)))
        proj_high, proj_low = halves(projected)
        first = mxu(jnp.concatenate([proj_high, proj_low], axis=1), high, dims(0, 0))
        second = mxu(proj_high, low, dims(0, 0))
        wide = first if wide is None else wide + first
        narrow = second if narrow is None else narrow + second
    total[...] = wide[:width, :] + (wide[width:, :] + narrow)
    share = width // len(part_refs)
    for k, ref in enumerate(part_refs):
        start = pl.multiple_of((me_ref[0] ^ k) * share, share)
        ref[...] = total[pl.ds(start, share), :]


def sketch_parts(me, here, count, flat, omega):
    rows, cells = flat.shape
    width = omega.shape[1]
    far = pl.BlockSpec(memory_space=pltpu.HBM)
    out = pl.pallas_call(
        sketch_kernel,
        in_specs=[SMEM, SMEM, far, far],
        out_specs=[VMEM] * (1 + count),
        out_shape=[pltpu.VMEM((rows, cells), jnp.float32)]
        + [pltpu.VMEM((width // count, cells), jnp.float32)] * count,
        scratch_shapes=[
            pltpu.VMEM((cells, width), jnp.float32),
            pltpu.VMEM((width, cells), jnp.float32),
            pltpu.SemaphoreType.DMA((PIECES + 1,)),
        ],
        compiler_params=pltpu.CompilerParams(vmem_limit_bytes=24 << 20),
        name="sketch",
    )(me, here, *[pltpu.with_memory_space_constraint(x, pltpu.HBM) for x in (flat, omega)])
    return out[0], out[1:]


def gather_sketch(scale, me_ref, piece_refs, whole):
    share = piece_refs[0].shape[0]
    for k, ref in enumerate(piece_refs):
        start = pl.multiple_of((me_ref[0] ^ k) * share, share)
        whole[pl.ds(start, share), :] = ref[...] * scale
    return whole[...]


def chunk_kernel(scale, step, many, here_ref, field_ref, *refs):
    piece_refs, out_ref = refs[:many], refs[-1]
    sketch = jnp.concatenate([ref[...] for ref in piece_refs], axis=0) * scale
    count = sketch.shape[0]
    rows, _, cells = field_ref.shape
    share = out_ref.shape[1] // rows
    start = pl.multiple_of((here_ref[0] ^ step) * share, share)
    high, low = halves(field_ref[:, pl.ds(start, share), :].reshape(rows * share, cells))
    sketch_high, sketch_low = halves(sketch)
    both = mxu(jnp.concatenate([sketch_high, sketch_low], axis=0), high, dims(1, 1))
    out_ref[...] = both[:count] + (both[count:] + mxu(sketch_high, low, dims(1, 1)))


def field_chunk(scale, step, here, field, pieces, share, after):
    kernel = functools.partial(chunk_kernel, scale, step, len(pieces))
    shape = (sum(piece.shape[0] for piece in pieces), field.shape[0] * share)
    return kernel_call(kernel, "chunk", shape, [here], [field] + pieces + after)


def lift_kernel(planes, share, count, inverse_ref, *refs):
    out_ref = refs[-1]
    inv_high, inv_low = halves(inverse_ref[...])
    width = inv_high.shape[1]
    high, low = halves(jnp.concatenate([ref[...] for ref in refs[:count]], axis=0))
    both = mxu(high, jnp.concatenate([inv_high, inv_low], axis=1), dims(0, 0))
    value = both[:, :width] + (both[:, width:] + mxu(low, inv_high, dims(0, 0)))
    value = jnp.swapaxes(value.reshape(planes, out_ref.shape[0], share, width), 1, 2)
    for v in range(planes):
        for z in range(share):
            at = (v * share + z) * width
            out_ref[:, at:at + width] = value[v, z]


def lift(planes, share, inverse, chunk, after):
    samples, width = chunk[0].shape[1], inverse.shape[1]
    shape = (samples // (planes * share), planes * share * width)
    kernel = functools.partial(lift_kernel, planes, share, len(chunk))
    return kernel_call(kernel, "lift", shape, [], [inverse] + chunk + after)


def gram_kernel(planes, share_z, order, count, me_ref, omega_ref, inverse_ref, *refs):
    chunk_refs, early = refs[:count], refs[count:-4]
    part_ref, last_ref, rows_ref, cols_ref = refs[-4:]
    lift_kernel(planes, share_z, count, inverse_ref, *chunk_refs, last_ref)
    slab_refs = [None] * (len(order))
    for k, ref in zip(order, [*early, last_ref]):
        slab_refs[k] = ref
    share = slab_refs[0].shape[0]
    high, low = halves(jnp.concatenate([ref[...] for ref in slab_refs], axis=0))
    rows_ref[...] = mxu(high, high, dims(1, 1)) + (mxu(high, low, dims(1, 1)) + mxu(low, high, dims(1, 1)))
    for ref, out in ((rows_ref, cols_ref), (cols_ref, rows_ref)):
        value = ref[...].T
        for k in range(len(slab_refs)):
            start = pl.multiple_of((me_ref[0] ^ k) * share, share)
            out[pl.ds(start, share), :] = value[k * share:(k + 1) * share, :]
    part_ref[...] = exact(rows_ref[...], omega_ref[...], dims(1, 1))


def mix_kernel(which, me_ref, factor_ref, *refs):
    count = factor_ref.shape[0] // refs[0].shape[0]
    slab_refs, out_refs, mixed = refs[:count], refs[-1 - len(which):-1], refs[-1]
    planes, share_k, share_z, width = out_refs[0].shape
    rows_y = slab_refs[0].shape[0]
    own = [factor_ref[pl.ds(pl.multiple_of((me_ref[0] ^ k) * rows_y, rows_y), rows_y), :] for k in range(count)]
    fac_high, fac_low = halves(jnp.concatenate(own, axis=0))
    high, low = halves(jnp.concatenate([ref[...] for ref in slab_refs], axis=0))
    mixed[...] = mxu(fac_high, high, dims(0, 0)) + (mxu(fac_high, low, dims(0, 0)) + mxu(fac_low, high, dims(0, 0)))
    for k, ref in zip(which, out_refs):
        start = pl.multiple_of((me_ref[0] ^ k) * share_k, share_k)
        block = mixed[pl.ds(start, share_k), :]
        for v in range(planes):
            at = lambda z: (v * share_z + z) * width
            rows = jnp.stack([block[:, at(z):at(z) + width] for z in range(share_z)], axis=0)
            ref[v] = jnp.swapaxes(rows, 0, 1)


def last_kernel(divisor, which, count, rank_ref, me_ref, *refs):
    parts, slabs, blocks = refs[:count], refs[count:2 * count], refs[2 * count + 1:-2]
    factor_ref, inverse, mixed = refs[2 * count], refs[-2], refs[-1]
    factor_y_kernel(divisor, rank_ref, *parts, factor_ref, inverse)
    mix_kernel(which, me_ref, factor_ref, *slabs, *blocks, mixed)


def place_kernel(order, me_ref, *refs):
    *piece_refs, out_hbm, placed = refs
    share = piece_refs[0].shape[2]
    copies = []
    for k, ref in zip(order, piece_refs):
        start = pl.multiple_of((me_ref[0] ^ k) * share, share)
        copy = pltpu.make_async_copy(ref, out_hbm.at[:, :, pl.ds(start, share), :], placed.at[k])
        copy.start()
        copies.append(copy)
    for copy in copies:
        copy.wait()


def place(me, pieces, shape):
    order = steps(len(pieces)) + [0]
    return pl.pallas_call(
        functools.partial(place_kernel, order),
        in_specs=[SMEM] + [VMEM] * len(pieces),
        out_specs=pl.BlockSpec(memory_space=pltpu.HBM),
        out_shape=jax.ShapeDtypeStruct(shape, jnp.float32),
        scratch_shapes=[pltpu.SemaphoreType.DMA((len(pieces),))],
        compiler_params=pltpu.CompilerParams(vmem_limit_bytes=16 << 20),
        name="place",
    )(me, *[held(pieces[k]) for k in order])


def eliminate(gram, count, rank, out_ref):
    lanes = lax.broadcasted_iota(jnp.int32, (8, count), 1)
    subs = lax.broadcasted_iota(jnp.int32, (8, count), 0)
    blocks = count // 8
    full = lambda x: jnp.broadcast_to(x, (8, count))
    left = [gram[8 * b:8 * b + 8, :] for b in range(blocks)]
    right = [(lanes == subs + 8 * b).astype(jnp.float32) for b in range(blocks)]
    for b in range(blocks):
        at = 8 * b
        l = [full(left[b][k:k + 1, :]) for k in range(8)]
        r = [full(right[b][k:k + 1, :]) for k in range(8)]
        a = {(k, m): full(l[k][:, at + m:at + m + 1]) for k in range(8) for m in range(k, 8)}
        inv, f = {}, {}
        for k in range(8):
            inv[k] = 1.0 / a[k, k]
            for m in range(k + 1, 8):
                f[k, m] = a[k, m] * inv[k]
                for q in range(m, 8):
                    a[m, q] = a[m, q] - f[k, m] * a[k, q]
                l[m] = l[m] - f[k, m] * l[k]
                r[m] = r[m] - f[k, m] * r[k]
            row = (r[k] * lax.rsqrt(a[k, k]))[0:1]
            out_ref[at + k:at + k + 1, :] = jnp.where(at + k < rank, row, 0.0)
        if b + 1 == blocks:
            break
        w, v = {}, {}
        for k in reversed(range(8)):
            w[k], v[k] = l[k] * inv[k], r[k] * inv[k]
            for m in range(k + 1, 8):
                w[k] = w[k] - f[k, m] * w[m]
                v[k] = v[k] - f[k, m] * v[m]
        for i in range(b + 1, blocks):
            column = [full(left[i][:, at + k:at + k + 1]) for k in range(8)]
            for k in range(8):
                left[i] = left[i] - column[k] * w[k]
                right[i] = right[i] - column[k] * v[k]


def factor_x_kernel(scale, rank_ref, me_ref, *refs):
    *piece_refs, out_ref, sketch_ref, inverse_ref = refs
    sketch_t = gather_sketch(scale, me_ref, piece_refs, sketch_ref)
    eliminate(exact(sketch_t, sketch_t, dims(1, 1)), sketch_t.shape[0], rank_ref[0], inverse_ref)
    inverse_ref[...] = inverse_ref[...].T
    share = piece_refs[0].shape[0]
    for k in range(len(piece_refs)):
        start = pl.multiple_of((me_ref[0] ^ k) * share, share)
        out_ref[k * share:(k + 1) * share, :] = inverse_ref[pl.ds(start, share), :]


def inverse_factor_x(scale, rank, me, pieces):
    width = pieces[0].shape[0] * len(pieces)
    scratch = [pltpu.VMEM((width, pieces[0].shape[1]), jnp.float32), pltpu.VMEM((width, width), jnp.float32)]
    kernel = functools.partial(factor_x_kernel, scale)
    return kernel_call(kernel, "factor_x", (width, width), [rank, me], pieces, scratch)


def apply_kernel(scale, inverse_ref, *refs):
    *piece_refs, out_ref = refs
    sketch = jnp.concatenate([ref[...] for ref in piece_refs], axis=0) * scale
    out_ref[...] = exact(sketch, inverse_ref[...], dims(0, 0))


def make_factor_x(scale, inverse, pieces):
    shape = (pieces[0].shape[1], inverse.shape[1])
    kernel = functools.partial(apply_kernel, scale)
    return kernel_call(kernel, "apply", shape, [], [inverse] + pieces, whole_out=True)


def factor_y_kernel(divisor, rank_ref, *refs):
    *part_refs, out_ref, inverse = refs
    sketch = part_refs[0][...]
    for ref in part_refs[1:]:
        sketch = sketch + ref[...]
    sketch = sketch / divisor
    eliminate(exact(sketch, sketch, dims(0, 0)), sketch.shape[1], rank_ref[0], inverse)
    out_ref[...] = exact(sketch, inverse[...], dims(1, 1))


def make_factor_y(rank, parts, divisor):
    width = parts[0].shape[1]
    scratch = [pltpu.VMEM((width, width), jnp.float32)]
    kernel = functools.partial(factor_y_kernel, divisor)
    return kernel_call(kernel, "factor_y", parts[0].shape, [rank], parts, scratch)


def body(field, omega_x, omega_y, rank_x, rank_y):
    planes, rows_y, rows_z, cells_x = field.shape
    ranks_x = omega_x.shape[1]
    ranks_y = omega_y.shape[1]
    n_gy = lax.axis_size("gy")
    gy = lax.axis_index("gy")
    all_planes = planes * lax.axis_size("vert")
    all_rows_y = rows_y * n_gy
    all_rows_z = rows_z * lax.axis_size("gz")
    flat = field.reshape(-1, cells_x)

    here = gy[None].astype(jnp.int32)
    quarter = lax.axis_index("gz") * lax.axis_size("vert") + lax.axis_index("vert")
    n_quarter = lax.axis_size(("gz", "vert"))
    quarter = quarter[None].astype(jnp.int32)
    field_v, parts = sketch_parts(quarter, here, n_quarter, flat, omega_x)
    pieces = sum_sketch(parts)
    scale = 1.0 / float(all_planes * all_rows_y * all_rows_z)

    share_z = rows_z // n_gy
    share_k = ranks_y // n_gy
    field_z = field_v.reshape(planes * rows_y, rows_z, cells_x)
    tiled = share_z % 8 == 0 and share_k % 8 == 0 and n_gy == 4 and n_quarter == 4
    inverse_x = inverse_factor_x(scale, rank_x, quarter, pieces)
    order = steps(n_gy)
    chunks = [[] for _ in range(n_gy)]
    if tiled:
        after, ahead = [], []
        for s in order:
            if s & 2:
                part = field_chunk(scale, s, here, field_z, pieces[:2], share_z, after)
                after = [part]
                chunks[s].append(swap(part, "gy", s))
                ahead.append(chunks[s][0])
        for s in [2, 1, 0, 3]:
            wait = ahead + [inverse_x] if s == 3 else []
            part = field_chunk(scale, s, here, field_z, pieces[2 * len(chunks[s]):], share_z, after + wait)
            after = [part]
            chunks[s].append(swap(part, "gy", s) if s else part)
    else:
        sketch = jnp.concatenate(pieces, axis=0) * scale
        raw = lax.dot_general(flat, sketch, dims(1, 1), precision=HIGHEST)
        raw = raw.reshape(planes * rows_y, rows_z, ranks_x)
        for s in order + [0]:
            chunk = lax.dynamic_slice_in_dim(raw, (gy ^ s) * share_z, share_z, 1)
            chunks[s] = swap(chunk, "gy", s) if s else chunk

    factor_x = make_factor_x(scale, inverse_x, pieces)

    if tiled:
        slabs = [None] * n_gy
        after = []
        for s in ([0] + order)[:-1]:
            slabs[s] = lift(planes, share_z, inverse_x, chunks[s], after)
            after = [slabs[s]]
        scratch = [pltpu.VMEM((all_rows_y, all_rows_y), jnp.float32)] * 2
        last = order[-1]
        kernel = functools.partial(gram_kernel, planes, share_z, [0] + order, len(chunks[last]))
        values = [omega_y.T, inverse_x] + chunks[last] + [slabs[s] for s in [0] + order[:-1]]
        shapes = [(all_rows_y, ranks_y), slabs[0].shape]
        part_y, slabs[last] = kernel_call(kernel, "gram", shapes, [here], values, scratch)
    else:
        spread = jnp.stack(chunks).reshape(-1, ranks_x)
        spread = lax.dot_general(spread, inverse_x, dims(1, 0), precision=HIGHEST)
        spread = spread.reshape(n_gy, planes, rows_y, share_z, ranks_x)
        local_gram_y = jnp.einsum("gvazr,hvbzr->gahb", spread, spread, precision=HIGHEST)
        local_gram_y = local_gram_y.reshape(all_rows_y, all_rows_y)
        omega_p = by_step(omega_y.reshape(n_gy, rows_y, ranks_y), gy, n_gy).reshape(all_rows_y, ranks_y)
        part_y = jnp.dot(local_gram_y, omega_p, precision=HIGHEST)
        part_y = by_step(part_y.reshape(n_gy, rows_y, ranks_y), gy, n_gy).reshape(all_rows_y, ranks_y)
    for axis in ("vert", "gz"):
        count = lax.axis_size(axis)
        got = [swap(part_y, axis, s) for s in steps(count)]
        for other in got:
            part_y = part_y + other
    parts = [part_y] + [swap(part_y, "gy", s) for s in range(1, n_gy)]
    divisor = float(all_planes * all_rows_z * ranks_x)
    if tiled:
        shape = (planes, share_k, share_z, ranks_x)
        which = steps(n_gy) + [0]
        kernel = functools.partial(last_kernel, divisor, which, n_gy)
        shapes = [(all_rows_y, ranks_y)] + [shape] * n_gy
        scratch = [
            pltpu.VMEM((ranks_y, ranks_y), jnp.float32),
            pltpu.VMEM((ranks_y, planes * share_z * ranks_x), jnp.float32),
        ]
        factor_y, *blocks = kernel_call(kernel, "last", shapes, [rank_y, here], parts + slabs, scratch)
        pieces = [None] * n_gy
        for s, block in zip(which, blocks):
            pieces[s] = swap(block, "gy", s) if s else block
        core = place(here, pieces, (planes, share_k, rows_z, ranks_x))
        return (core, factor_x, factor_y)
    factor_y = make_factor_y(rank_y, parts, divisor)
    weights = by_step(factor_y.reshape(n_gy, rows_y, ranks_y), gy, n_gy)
    weights = weights.reshape(n_gy, rows_y, n_gy, share_k)
    weights = jnp.moveaxis(by_step(jnp.moveaxis(weights, 2, 0), gy, n_gy), 0, 2)
    mixed = jnp.einsum("gvyzr,gyhk->hvkzr", spread, weights, precision=HIGHEST)
    pieces = [None] * n_gy
    for s in steps(n_gy):
        pieces[s] = swap(mixed[s], "gy", s)
    pieces[0] = mixed[0]
    core = by_step(jnp.stack(pieces), gy, n_gy)
    core = jnp.moveaxis(core, 0, 2).reshape(planes, share_k, rows_z, ranks_x)
    return (core, factor_x, factor_y)


def solution(mesh):
    in_specs = (P(("grp", "vert"), "gy", "gz", None), P(), P(), P("grp"), P("grp"))
    out_specs = (P(("grp", "vert"), "gy", "gz", None), P("grp", None), P("grp", None))
    return jax.shard_map(body, mesh=mesh, in_specs=in_specs, out_specs=out_specs, check_vma=False)
```
